32 devices in a mesh: dp: 8 (over y, x, core), vocab: 4 (over z).
Axes of the slice: x: 2, y: 2, z: 4, core: 2. Of those that a mesh axis runs over, the one named last changes fastest.
Arguments:
- hidden: bfloat16 [128, 5120], P('dp', 'vocab')
- inputs: bfloat16 [128, 3072], P('dp', 'vocab'), may hold values from -6 to 6
- gain: float32 [5120], replicated, may hold values from 0.5 to 1.5
- unembed: bfloat16 [6400, 5120], P(('dp', 'vocab'))
- proj_out: bfloat16 [5120, 128], replicated, may hold values from -6 to 6
- proj_in: bfloat16 [3072, 128], replicated, may hold values from -0.109375 to 0.109375
- targets: int32 [128], replicated, may hold values from 0 to 6399
- segment_ids: int32 [128], replicated, may hold values from 0 to 3, never falling along the last dimension, each value on 1 to 96 neighbouring positions
- store: bfloat16 [2048, 16384], P(('dp', 'vocab')), may hold values from -0.005859375 to 0.005859375
Outputs:
- scores: float32 [4, 2048], P(None, ('dp', 'vocab'))
- logprob: float32 [128], P('dp')
The draws below stay inside these ranges and needn't reach their ends.
Inputs may be any that keep to these rules, and one draw needn't show every extreme that they name: `segment_ids`: each sequence is a run of consecutive tokens; ids never fall; each sequence has 1 to 96 tokens and one has exactly 96.
All inputs are finite; a program needn't handle non-finite values.
Results may differ from the reference program's by a relative error of at most 0.0074.
Values may be sent and summed in bfloat16 or wider, within the bound.
No kernel may reach another device: no remote copies, remote signals or barrier semaphores. Data moves between devices by JAX's collectives and lax.ppermute only.
A program may use at most 64 MiB of HBM per device.

```python
import math
import jax
import jax.numpy as jnp
import numpy as np
from jax import lax

D = 5120
FIN = 3072
PROJ = 128
L = 96
Q = 128
S = 4
V = 6400
E = 2048
F = 16384


PAIR_SCALE = [340.0, 500.0, 680.0, 850.0]


BLEND_LEVELS = [1.5, 1.0, 0.5, 0.0]


ROW_FACTOR = [4.0, 8.0, 16.0, 8.0]


def unembed_rows(key, row_ids):
    base_key = jax.random.fold_in(key, 11)

    def one_row(row_id):
        return jax.random.normal(jax.random.fold_in(base_key, row_id), (D,), jnp.float32)
    return jnp.clip(jax.vmap(one_row)(row_ids), -5.0, 5.0) * (5.0 / math.sqrt(D))


def picked_rows(key):
    return jax.random.permutation(jax.random.fold_in(key, 31), V)[:8].astype(jnp.int32)


def draw_unembed(key, part):
    row_ids = jnp.arange(V, dtype=jnp.int32)
    rows = unembed_rows(key, row_ids)
    picked = picked_rows(key)
    picked_scale = jnp.repeat(jnp.array(PAIR_SCALE, jnp.float32), 2)
    matches = row_ids[:, None] == picked[None, :]
    special = jnp.any(matches, axis=1)
    row_scale = jnp.sum(jnp.where(matches, picked_scale[None, :], jnp.zeros_like(picked_scale)[None, :]), axis=1)
    lengths = jnp.sqrt(jnp.sum(rows * rows, axis=1, keepdims=True))
    boosted = rows / lengths * (row_scale[:, None] / math.sqrt(D))
    rows = jnp.where(special[:, None], boosted, rows)
    return rows.astype(jnp.bfloat16)


def draw_hidden(key, part):
    base_key = jax.random.fold_in(key, 23)
    noise_key = jax.random.fold_in(base_key, 0)
    pick_key = jax.random.fold_in(base_key, 3)
    mix_key = jax.random.fold_in(base_key, 4)
    extra_key = jax.random.fold_in(base_key, 5)
    values = jnp.clip(jax.random.normal(noise_key, (Q, D), jnp.float32), -4.0, 4.0)
    picked = picked_rows(key)
    directions = unembed_rows(key, picked)
    directions = directions / jnp.linalg.norm(directions, axis=1, keepdims=True) * 5.0
    pair_scale = jnp.array(PAIR_SCALE, jnp.float32)
    blend_scale = jnp.array(BLEND_LEVELS, jnp.float32)
    row_factor = jnp.array(ROW_FACTOR, jnp.float32)
    top_gap = jax.random.uniform(mix_key, (4,), jnp.float32, 1.2, 2.8)
    mix_ratio = 1.0 + top_gap * jnp.sqrt(2.0 + blend_scale * blend_scale) / pair_scale
    extra = jnp.clip(jax.random.normal(extra_key, (4, D), jnp.float32), -4.0, 4.0) * (5.0 / math.sqrt(D))
    aligned = directions[0::2] + mix_ratio[:, None] * directions[1::2] + blend_scale[:, None] * extra
    aligned = aligned * row_factor[:, None]
    positions = jax.random.permutation(pick_key, Q)[:4].astype(jnp.int32)
    values = values.at[positions].set(aligned)
    return values.astype(jnp.bfloat16)


def set_ends(drawn, own_key, low, largest):
    index_at = [jax.random.randint(jax.random.fold_in(own_key, axis), (), 0, length) for axis, length in enumerate(drawn.shape)]
    main_axis = drawn.shape.index(max(drawn.shape))
    next_to = index_at[:main_axis] + [(index_at[main_axis] + 1) % drawn.shape[main_axis]] + index_at[main_axis + 1:]
    return drawn.at[tuple(index_at)].set(low).at[tuple(next_to)].set(largest)


def block_scale(rng, dims, cuts, low, high):
    level, own = 1.0, jax.random.fold_in(rng, 6)
    for axis_at, parts in cuts:
        heights = jnp.exp(jax.random.uniform(jax.random.fold_in(own, axis_at), (parts,), jnp.float32, low / len(cuts), high / len(cuts)))
        level = level * jnp.repeat(heights, dims[axis_at] // parts).reshape([-1 if axis == axis_at else 1 for axis in range(len(dims))])
    return level


def split_up(count, total, limit, slope):
    weights = [(1 << 20) // math.isqrt(rank ** slope) + 1 for rank in range(2, count + 1)]
    rest, holding = total - limit - (count - 1), [1] * (count - 1)
    while rest > 0:
        free = [i for i in range(count - 1) if holding[i] < limit]
        pool, left = sum([weights[i] for i in free]), rest
        for i in free:
            more = min(limit - holding[i], max(1, left * weights[i] // pool), rest)
            holding[i] = holding[i] + more
            rest = rest - more
    return np.array([limit] + holding)


def ragged_sizes(stream_key, amount, total, most, skew):
    if amount == 2:
        one = jax.random.randint(stream_key, (), max(1, total - most), min(most, total - 1) + 1)
        return jnp.stack([one, total - one])
    sizes = jnp.asarray(split_up(amount, total, most, skew), jnp.int32)
    twos = (amount - 1) // 2
    donor, receiver = sizes[1:1 + 2 * twos:2], sizes[2:2 + 2 * twos:2]
    room = jnp.minimum(donor - 1, most - receiver)
    moved = jax.random.randint(jax.random.fold_in(stream_key, 1), (twos,), 0, 1 << 20) % (room + 1)
    sizes = sizes.at[1:1 + 2 * twos:2].set(donor - moved).at[2:2 + 2 * twos:2].set(receiver + moved)
    return sizes[jax.random.permutation(jax.random.fold_in(stream_key, 2), amount)]


def gaussian(key, extent, scale, limit, cuts=(), kind=jnp.bfloat16):
    values = scale * jax.random.normal(key, extent, jnp.float32)
    if cuts:
        values = values * block_scale(key, extent, cuts, -0.22, 0.18)
    return jnp.clip(values, -limit, limit).astype(kind)


def setup_inputs(seed: int = 0) -> dict:
    keys = jax.random.split(jax.random.key(seed), 10)
    return {
        "hidden": draw_hidden(jax.random.fold_in(keys[9], 71), 0),
        "inputs": gaussian(keys[1], (Q, FIN), 1.0, 6.0, ((0, 8), (1, 4))),
        "gain": jnp.clip(1.0 + 0.1 * jax.random.normal(keys[2], (D,), jnp.float32), 0.5, 1.5),
        "unembed": draw_unembed(jax.random.fold_in(keys[9], 71), 0),
        "proj_out": gaussian(keys[4], (D, PROJ), 1.0, 6.0),
        "proj_in": gaussian(keys[5], (FIN, PROJ), FIN ** -0.5, 0.109375),
        "targets": set_ends(jax.random.randint(keys[6], (Q,), 0, V), jax.random.fold_in(keys[6], 1), 0, V - 1).astype(jnp.int32),
        "segment_ids": jnp.searchsorted(jnp.cumsum(ragged_sizes(keys[7], S, Q, L, 0)), jnp.arange(Q), side="right").astype(jnp.int32),
        "store": gaussian(keys[8], (E, F), (64 * F) ** -0.5, 0.005859375, ((0, 32),)),
    }


EPSILON = 1e-06

def reference(hidden, inputs, gain, unembed, proj_out, proj_in, targets, segment_ids, store):
    hidden_f32 = hidden.astype(jnp.float32)
    root_mean = jnp.sqrt(lax.optimization_barrier(jnp.mean(hidden_f32 * hidden_f32, axis=1)) + EPSILON)
    normed = (hidden_f32 * gain[None, :] / root_mean[:, None]).astype(jnp.bfloat16)
    logits = lax.dot_general(normed.astype(jnp.float32), unembed.astype(jnp.float32), (((1,), (1,)), ((), ())), preferred_element_type=jnp.float32)
    row_peak = lax.optimization_barrier(jnp.max(logits, axis=1))
    shifted = jnp.exp(logits - row_peak[:, None])
    row_total = lax.optimization_barrier(jnp.sum(shifted, axis=1))
    column_ids = jnp.arange(V, dtype=jnp.int32)
    onehot = targets[:, None] == column_ids[None, :]
    target_logit = lax.optimization_barrier(jnp.sum(jnp.where(onehot, logits, jnp.zeros_like(logits)), axis=1))
    logprob = target_logit - row_peak - jnp.log(row_total)
    dlogits = (onehot.astype(jnp.float32) - shifted / row_total[:, None]).astype(jnp.bfloat16)
    dnormed = jnp.dot(dlogits.astype(jnp.float32), unembed.astype(jnp.float32), preferred_element_type=jnp.float32)
    weighted = dnormed * gain[None, :]
    grad_proj = jnp.dot(weighted, proj_out.astype(jnp.float32), precision=lax.Precision.HIGHEST)
    grad_dot = lax.optimization_barrier(jnp.sum(weighted * hidden_f32, axis=1))
    hidden_proj = jnp.dot(hidden.astype(jnp.float32), proj_out.astype(jnp.float32), preferred_element_type=jnp.float32)
    out_grad = grad_proj / root_mean[:, None] - hidden_proj * (grad_dot / (D * root_mean ** 3))[:, None]
    in_proj = jnp.dot(inputs.astype(jnp.float32), proj_in.astype(jnp.float32), preferred_element_type=jnp.float32)
    member = (segment_ids[:, None] == jnp.arange(S, dtype=jnp.int32)[None, :]).astype(jnp.float32)
    spread = (member[:, :, None] * out_grad[:, None, :]).reshape(Q, S * PROJ)
    seq_grads = lax.dot_general(spread, in_proj, (((0,), (0,)), ((), ())), precision=lax.Precision.HIGHEST)
    seq_grads = seq_grads.reshape(S, PROJ * PROJ).astype(jnp.bfloat16)
    scores = lax.dot_general(seq_grads.astype(jnp.float32), store.astype(jnp.float32), (((1,), (1,)), ((), ())), preferred_element_type=jnp.float32)
    return (scores, logprob)
```

```python
import functools

import jax
import jax.numpy as jnp
from jax import lax
from jax.experimental import pallas as pl
from jax.experimental.pallas import tpu as pltpu
from jax.sharding import PartitionSpec as P

EPSILON = 1e-06
AXES = ("dp", "vocab")
F32 = jnp.float32
BF16 = jnp.bfloat16


VMEM = pl.BlockSpec(memory_space=pltpu.VMEM)
ANY = pl.BlockSpec(memory_space=pl.ANY)


def split(x):
    high = x.astype(BF16)
    return high, (x - high.astype(F32)).astype(BF16)


def dot(a, b, dims=((1,), (0,))):
    return lax.dot_general(a, b, (dims, ((), ())), preferred_element_type=F32)


def call(kernel, out_shape, n_in, any_at=(), scratch=(), name=None):
    specs = [ANY if i in any_at else VMEM for i in range(n_in)]
    outs = jax.tree.map(lambda _: VMEM, out_shape)
    return pl.pallas_call(
        kernel, out_shape=out_shape, in_specs=specs, out_specs=outs, scratch_shapes=list(scratch), name=name
    )


def early_kernel(inputs, proj_in, unembed, gain, proj_out, weights, in_part):
    scaled_high, scaled_low = split(unembed[...].astype(F32) * gain[...])
    weights[...] = dot(scaled_high, proj_out[...]) + dot(scaled_low, proj_out[...])
    width = inputs.shape[1]
    start = pl.multiple_of(lax.axis_index("vocab") * width, 16)
    part = dot(inputs[...], proj_in[pl.ds(start, width), :])
    chunks, rows, _ = in_part.shape
    for c in range(chunks):
        in_part[c] = part[c * rows : (c + 1) * rows]


def row_kernel(offsets, *refs):
    pieces, proj_out, aux = refs[:-2], refs[-2], refs[-1]
    total, squares, features = 0.0, 0.0, 0
    for piece, (rows, start_of) in zip(pieces, offsets, strict=True):
        for k in range(piece.shape[0] // rows):
            block = piece[k * rows : (k + 1) * rows, :]
            width = block.shape[1]
            start = pl.multiple_of(start_of(k), 16)
            total = total + dot(block, proj_out[pl.ds(start, width), :])
            wide = block.astype(F32)
            squares = squares + jnp.sum(wide * wide, axis=1, keepdims=True)
            features += width
    root_mean = jnp.sqrt(squares / features + EPSILON)
    root_mean = jnp.broadcast_to(root_mean, total.shape)
    chunks, rows, _ = aux.shape
    for c in range(chunks):
        aux[c, :, 0:128] = total[c * rows : (c + 1) * rows]
        aux[c, :, 128:256] = root_mean[c * rows : (c + 1) * rows]


def logits_kernel(layout, *refs):
    n = len(layout)
    pieces = refs[:n]
    unembed_hbm, gain, targets, weights, in_part, out, unembed, scaled, normed, squares, sem = refs[n:]
    copy = pltpu.make_async_copy(unembed_hbm, unembed, sem)
    copy.start()
    tokens, features = scaled.shape
    squares[...] = jnp.zeros_like(squares)
    for piece, blocks in zip(pieces, layout, strict=True):
        for row, rows, token_at, feature_at in blocks:
            block = piece[row : row + rows, :].astype(F32)
            width = block.shape[1]
            token = pl.multiple_of(token_at(), 16)
            feature = pl.multiple_of(feature_at(), 128)
            partial = jnp.sum(block * block, axis=1, keepdims=True)
            squares[pl.ds(token, rows), :] += jnp.broadcast_to(partial, (rows, 128))
            scaled[pl.ds(token, rows), pl.ds(feature, width)] = block * gain[:, pl.ds(feature, width)]
    inverse = 1.0 / jnp.sqrt(squares[...] / features + EPSILON)
    normed[...] = (scaled[...] * inverse[:, 0:1]).astype(BF16)
    copy.wait()
    logits = dot(normed[...], unembed[...], ((1,), (1,)))
    entries = logits.shape[1]
    place = lax.axis_index("dp") * lax.axis_size("vocab") + lax.axis_index("vocab")
    column = lax.broadcasted_iota(jnp.int32, logits.shape, 1) + place * entries
    onehot = targets[...] == column
    peak = jnp.max(logits, axis=1, keepdims=True)
    shifted = logits - peak
    other = jnp.where(onehot, 0.0, jnp.exp(shifted))
    total = jnp.sum(other, axis=1, keepdims=True)
    moment = jnp.sum(other * shifted, axis=1, keepdims=True)
    target_logit = jnp.sum(jnp.where(onehot, logits, 0.0), axis=1, keepdims=True)
    w_high, w_low = split(weights[...])
    p_high, p_low = split(other)
    sums = dot(p_high, w_high) + (dot(p_high, w_low) + dot(p_low, w_high))
    hot = onehot.astype(F32).astype(BF16)
    target_row = dot(hot, w_high) + dot(hot, w_low)
    lane = lax.broadcasted_iota(jnp.int32, (tokens, 128), 1)
    stats = jnp.where(
        lane < 64, jnp.where(lane < 32, peak, total), jnp.where(lane < 96, moment, target_logit)
    )
    chunks, rows, _ = out.shape
    for c in range(chunks):
        here = slice(c * rows, (c + 1) * rows)
        out[c, :, 0:128] = sums[here]
        out[c, :, 128:256] = target_row[here]
        out[c, :, 256:384] = stats[here]
    out[:, :, 384:512] = jnp.zeros((chunks, rows, 128), F32)
    own = in_part.shape[0]
    out[pl.ds(lax.axis_index("dp") * own, own), :, 384:512] = in_part[...]


def merge_kernel(features, parts, aux, out):
    index = lax.axis_index("vocab")
    hidden_proj = aux[index, :, 0:128]
    root_mean = aux[index, :, 128:256]
    stats = parts[:, :, 256:384]
    peak, total = stats[:, :, 0:1], stats[:, :, 32:33]
    moment, target_logit = stats[:, :, 64:65], jnp.sum(stats[:, :, 96:97], axis=0)
    row_peak = jnp.max(peak, axis=0)
    scale = jnp.exp(peak - row_peak[None])
    row_total = jnp.sum(scale * total, axis=0) + jnp.exp(target_logit - row_peak)
    weight = scale / row_total[None]
    rest = jnp.sum(weight * total, axis=0)
    target_row = jnp.sum(parts[:, :, 128:256], axis=0)
    grad_proj = rest * target_row - jnp.sum(weight * parts[:, :, 0:128], axis=0)
    slope = jnp.sum(weight * (total * (target_logit[None] - peak) - moment), axis=0)
    grad_dot = root_mean * slope
    out_grad = grad_proj / root_mean - hidden_proj * (
        grad_dot / (features * (root_mean * root_mean * root_mean))
    )
    logprob = target_logit - row_peak - jnp.log(row_total)
    in_proj = jnp.sum(parts[:, :, 384:512], axis=0)
    rows = out_grad.shape[0]
    lane = lax.broadcasted_iota(jnp.int32, (rows, 128), 1)
    token = lax.broadcasted_iota(jnp.int32, (rows, 128), 0) + index * rows
    spread = jnp.where(lane == token, logprob, 0.0)
    chunks = out.shape[0]
    for at, value in ((0, out_grad), (128, in_proj), (256, spread)):
        out[:, :, at : at + 128] = jnp.broadcast_to(value[None], (chunks, rows, 128))


def scores_kernel(parts, segments, store_hbm, scores, logprob, store, out_grad, in_proj, spread_high, spread_low, flat, sem):
    copy = pltpu.make_async_copy(store_hbm, store, sem)
    copy.start()
    chunks, rows, _ = parts.shape
    for c in range(chunks):
        here = slice(c * rows, (c + 1) * rows)
        out_grad[here, :] = parts[c, :, 0:128]
        in_proj[here, :] = parts[c, :, 128:256]
    own = lax.axis_size("vocab")
    own_part = parts[pl.ds(lax.axis_index("dp") * own, own), :, 256:384]
    own_part = jnp.sum(jnp.sum(own_part, axis=0), axis=0, keepdims=True)
    logprob[...] = own_part[:, 0 : logprob.shape[1]]
    turned = out_grad[...].T
    t_high = turned.astype(BF16).astype(F32)
    t_low = turned - t_high
    tokens = turned.shape[1]
    seqs = flat.shape[0]
    member = (segments[...] == lax.broadcasted_iota(jnp.int32, (seqs, tokens), 0)).astype(F32)
    for p in range(turned.shape[0]):
        spread_high[p * seqs : (p + 1) * seqs, :] = t_high[p : p + 1, :] * member
        spread_low[p * seqs : (p + 1) * seqs, :] = t_low[p : p + 1, :] * member
    i_high, i_low = split(in_proj[...])
    s_high, s_low = spread_high[...].astype(BF16), spread_low[...].astype(BF16)
    grads = dot(s_high, i_high) + (dot(s_high, i_low) + dot(s_low, i_high))
    width = grads.shape[1]
    for p in range(turned.shape[0]):
        flat[:, p * width : (p + 1) * width] = grads[p * seqs : (p + 1) * seqs, :]
    copy.wait()
    result = dot(flat[...].astype(BF16), store[...], ((1,), (1,)))
    scores[...] = result[0 : scores.shape[0], :]


def swap(x, size, mask):
    vocab = size["vocab"]
    count = size["dp"] * vocab
    return lax.ppermute(x, AXES, [(i, i ^ mask) for i in range(count)])


def body(size, hidden, inputs, gain, unembed, proj_out, proj_in, targets, segment_ids, store):
    n_dp, n_vocab = size["dp"], size["vocab"]
    devices = n_dp * n_vocab
    tokens, features = targets.shape[0], gain.shape[0]
    per_device = tokens // devices
    rows, width = hidden.shape
    seqs = tokens // 32
    entries = unembed.shape[0]
    projected = proj_out.shape[1]
    gain_row = gain.reshape(1, features)

    def mine(axis):
        return lambda: lax.axis_index(axis)

    if n_dp == 8 and n_vocab == 4 and width % 128 == 0:
        row_block = jnp.concatenate([hidden] + [swap(hidden, size, k) for k in range(1, n_vocab)], axis=0)
        row_offsets = ((rows, lambda k: (lax.axis_index("vocab") ^ k) * width),)
        row_pieces = (row_block,)
        near = {0: row_block}
        for r in (2, 4, 6):
            near[r] = swap(row_block, size, r * n_vocab)
        pieces = dict(near)
        for r in (0, 2, 4, 6):
            pieces[r + 1] = swap(near[r], size, n_vocab)
        layout = tuple(
            tuple(
                (
                    k * rows,
                    rows,
                    lambda r=r: (lax.axis_index("dp") ^ r) * rows,
                    lambda k=k: (lax.axis_index("vocab") ^ k) * width,
                )
                for k in range(n_vocab)
            )
            for r in range(n_dp)
        )
        pieces = [pieces[r] for r in range(n_dp)]
    else:
        row_block = lax.all_gather(hidden, "vocab", axis=1, tiled=True)
        row_offsets = ((rows, lambda k: 0),)
        row_pieces = (row_block,)
        pieces = [lax.all_gather(row_block, "dp", axis=0, tiled=True)]
        layout = (((0, tokens, lambda: 0, lambda: 0),),)

    sds = jax.ShapeDtypeStruct
    weights, in_part = call(
        early_kernel,
        (sds((entries, projected), F32), sds((n_vocab, per_device, projected), F32)),
        5,
        name="early",
    )(inputs, proj_in, unembed, gain_row, proj_out)
    aux = call(
        functools.partial(row_kernel, row_offsets),
        sds((n_vocab, per_device, 256), F32),
        len(row_pieces) + 1,
        name="row",
    )(*row_pieces, proj_out)
    partial = call(
        functools.partial(logits_kernel, layout),
        sds((devices, per_device, 512), F32),
        len(pieces) + 5,
        any_at=(len(pieces),),
        scratch=(
            pltpu.VMEM(unembed.shape, BF16),
            pltpu.VMEM((tokens, features), F32),
            pltpu.VMEM((tokens, features), BF16),
            pltpu.VMEM((tokens, 128), F32),
            pltpu.SemaphoreType.DMA,
        ),
        name="logits",
    )(*pieces, unembed, gain_row, targets.reshape(tokens, 1), weights, in_part)
    partial = lax.all_to_all(partial, AXES, 0, 0, tiled=True)
    merged = call(
        functools.partial(merge_kernel, features), sds((devices, per_device, 384), F32), 2, name="merge"
    )(partial, aux)
    merged = lax.all_to_all(merged, AXES, 0, 0, tiled=True)
    padded = -(-seqs // 8) * 8
    scores, logprob = call(
        scores_kernel,
        (sds((seqs, store.shape[0]), F32), sds((1, rows), F32)),
        3,
        any_at=(2,),
        scratch=(
            pltpu.VMEM(store.shape, BF16),
            pltpu.VMEM((tokens, projected), F32),
            pltpu.VMEM((tokens, projected), F32),
            pltpu.VMEM((projected * padded, tokens), F32),
            pltpu.VMEM((projected * padded, tokens), F32),
            pltpu.VMEM((padded, store.shape[1]), F32),
            pltpu.SemaphoreType.DMA,
        ),
        name="scores",
    )(merged, segment_ids.reshape(1, tokens), store)
    return scores, logprob.reshape(rows)


def solution(mesh):
    size = dict(mesh.shape)
    in_specs = (
        P("dp", "vocab"),
        P("dp", "vocab"),
        P(),
        P(AXES, None),
        P(),
        P(),
        P(),
        P(),
        P(AXES, None),
    )
    out_specs = (P(None, AXES), P("dp"))
    return jax.shard_map(
        functools.partial(body, size), mesh=mesh, in_specs=in_specs, out_specs=out_specs, check_vma=False
    )
```

```python
import functools

import jax
import jax.numpy as jnp
from jax import lax
from jax.experimental import pallas as pl
from jax.experimental.pallas import tpu as pltpu
from jax.sharding import PartitionSpec as P

EPSILON = 1e-06
AXES = ("dp", "vocab")
F32 = jnp.float32
BF16 = jnp.bfloat16


VMEM = pl.BlockSpec(memory_space=pltpu.VMEM)
ANY = pl.BlockSpec(memory_space=pl.ANY)


def split(x):
    high = x.astype(BF16)
    return high, (x - high.astype(F32)).astype(BF16)


def dot(a, b, dims=((1,), (0,))):
    return lax.dot_general(a, b, (dims, ((), ())), preferred_element_type=F32)


def call(kernel, out_shape, n_in, any_at=(), scratch=(), name=None, us=1.0):
    specs = [ANY if i in any_at else VMEM for i in range(n_in)]
    outs = jax.tree.map(lambda _: VMEM, out_shape)
    return pl.pallas_call(
        kernel,
        out_shape=out_shape,
        in_specs=specs,
        out_specs=outs,
        scratch_shapes=list(scratch),
        name=name,
        cost_estimate=pl.CostEstimate(flops=0, transcendentals=0, bytes_accessed=int(us * 3_000_000)),
        compiler_params=pltpu.CompilerParams(vmem_limit_bytes=32 * 1024 * 1024),
    )


def early_kernel(inputs, proj_in, unembed, gain, proj_out, targets, weights, in_part, target_column):
    scaled_high, scaled_low = split(unembed[...].astype(F32) * gain[...])
    weights[...] = dot(scaled_high, proj_out[...]) + dot(scaled_low, proj_out[...])
    width = inputs.shape[1]
    start = pl.multiple_of(lax.axis_index("vocab") * width, 16)
    part = dot(inputs[...], proj_in[pl.ds(start, width), :])
    chunks, rows, _ = in_part.shape
    for c in range(chunks):
        in_part[c] = part[c * rows : (c + 1) * rows]
    tokens = targets.shape[1]
    target_column[...] = jnp.broadcast_to(targets[...].astype(F32), (128, tokens)).T


def row_kernel(offsets, *refs):
    pieces, proj_out, aux = refs[:-2], refs[-2], refs[-1]
    total, squares, features = 0.0, 0.0, 0
    for piece, (rows, start_of) in zip(pieces, offsets, strict=True):
        for k in range(piece.shape[0] // rows):
            block = piece[k * rows : (k + 1) * rows, :]
            width = block.shape[1]
            start = pl.multiple_of(start_of(k), 16)
            total = total + dot(block, proj_out[pl.ds(start, width), :])
            wide = block.astype(F32)
            squares = squares + jnp.sum(wide * wide, axis=1, keepdims=True)
            features += width
    root_mean = jnp.sqrt(squares / features + EPSILON)
    root_mean = jnp.broadcast_to(root_mean, total.shape)
    chunks, rows, _ = aux.shape
    for c in range(chunks):
        aux[c, :, 0:128] = total[c * rows : (c + 1) * rows]
        aux[c, :, 128:256] = root_mean[c * rows : (c + 1) * rows]


def logits_kernel(layout, *refs):
    n = len(layout)
    pieces = refs[:n]
    unembed_hbm, gain, target_column, weights, in_part, out, unembed, scaled, normed, squares, sem = refs[n:]
    copy = pltpu.make_async_copy(unembed_hbm, unembed, sem)
    copy.start()
    tokens, features = scaled.shape
    squares[...] = jnp.zeros_like(squares)
    for piece, blocks in zip(pieces, layout, strict=True):
        for row, rows, token_at, feature_at in blocks:
            block = piece[row : row + rows, :].astype(F32)
            width = block.shape[1]
            token = pl.multiple_of(token_at(), 16)
            feature = pl.multiple_of(feature_at(), 128)
            partial = jnp.sum(block * block, axis=1, keepdims=True)
            squares[pl.ds(token, rows), :] += jnp.broadcast_to(partial, (rows, 128))
            scaled[pl.ds(token, rows), pl.ds(feature, width)] = block * gain[:, pl.ds(feature, width)]
    inverse = 1.0 / jnp.sqrt(squares[...] / features + EPSILON)
    normed[...] = (scaled[...] * inverse[:, 0:1]).astype(BF16)
    copy.wait()
    logits = dot(normed[...], unembed[...], ((1,), (1,)))
    entries = logits.shape[1]
    place = lax.axis_index("dp") * lax.axis_size("vocab") + lax.axis_index("vocab")
    column = lax.broadcasted_iota(jnp.int32, logits.shape, 1) + place * entries
    onehot = target_column[:, 0:1] == column.astype(F32)
    peak = jnp.max(logits, axis=1, keepdims=True)
    shifted = logits - peak
    other = jnp.where(onehot, 0.0, jnp.exp(shifted))
    total = jnp.sum(other, axis=1, keepdims=True)
    moment = jnp.sum(other * shifted, axis=1, keepdims=True)
    target_logit = jnp.sum(jnp.where(onehot, logits, 0.0), axis=1, keepdims=True)
    w_high, w_low = split(weights[...])
    p_high, p_low = split(other)
    sums = dot(p_high, w_high) + (dot(p_high, w_low) + dot(p_low, w_high))
    hot = onehot.astype(F32).astype(BF16)
    target_row = dot(hot, w_high) + dot(hot, w_low)
    lane = lax.broadcasted_iota(jnp.int32, (tokens, 128), 1)
    which = (lane // 2) % 4
    stats = jnp.where(which < 2, jnp.where(which == 0, peak, total), jnp.where(which == 2, moment, target_logit))
    high = stats.astype(BF16).astype(F32)
    middle = (stats - high).astype(BF16).astype(F32)
    low = stats - high - middle
    piece = (lane // 8) % 4
    stats = jnp.where(piece == 0, high, jnp.where(piece == 1, middle, jnp.where(piece == 2, low, 0.0)))
    chunks, rows = out.shape[0], tokens // out.shape[0]
    own = in_part.shape[0]
    mine = lax.axis_index("dp")
    block = lax.broadcasted_iota(jnp.int32, (rows, 128), 1) // (128 // own)
    for d in range(chunks // own):
        row_stats = stats[d * own * rows : (d * own + 1) * rows]
        for k in range(1, own):
            c = d * own + k
            row_stats = jnp.where(block == k, stats[c * rows : (c + 1) * rows], row_stats)
        for k in range(own):
            c = d * own + k
            here = slice(c * rows, (c + 1) * rows)
            terms = jnp.where(mine == d, in_part[k], 0.0)
            out[c] = jnp.concatenate([sums[here], target_row[here], terms, row_stats], axis=0).astype(BF16)


def merge_kernel(features, parts, aux, out, logprob):
    index, own = lax.axis_index("vocab"), lax.axis_size("vocab")
    hidden_proj = aux[index, :, 0:128]
    root_mean = aux[index, :, 128:256]
    chunks, rows = parts.shape[0], hidden_proj.shape[0]
    received = parts[...].astype(F32)
    stats = received[:, 3 * rows : 4 * rows].reshape(chunks * rows, 128)
    stats = stats + pltpu.roll(stats, 128 - 8, 1) + pltpu.roll(stats, 128 - 16, 1)
    shape = (chunks, rows, 128)
    peak, total = stats.reshape(shape), pltpu.roll(stats, 128 - 2, 1).reshape(shape)
    moment = pltpu.roll(stats, 128 - 4, 1).reshape(shape)
    target_logit = jnp.sum(pltpu.roll(stats, 128 - 6, 1).reshape(shape), axis=0)
    row_peak = jnp.max(peak, axis=0)
    scale = jnp.exp(peak - row_peak[None])
    row_total = jnp.sum(scale * total, axis=0) + jnp.exp(target_logit - row_peak)
    weight = scale / row_total[None]
    rest = jnp.sum(weight * total, axis=0)
    slope = jnp.sum(weight * (total * (target_logit[None] - peak) - moment), axis=0)
    log_of = target_logit - row_peak - jnp.log(row_total)
    group = 128 // own
    lane = lax.broadcasted_iota(jnp.int32, (rows, 128), 1)
    row = lax.broadcasted_iota(jnp.int32, (rows, 128), 0)
    spread = jnp.zeros((rows, 128), F32)
    for k in range(own):
        spread = jnp.where(lane == k * rows + row, log_of[:, k * group : k * group + 1], spread)
    logprob[...] = jnp.sum(spread, axis=0, keepdims=True)[:, 0 : logprob.shape[1]]

    def pick(x):
        at = lax.broadcasted_iota(jnp.int32, x.shape, x.ndim - 1) == index * group
        return jnp.sum(jnp.where(at, x, 0.0), axis=-1, keepdims=True)

    weight, rest, slope = pick(weight), pick(rest), pick(slope)
    target_row = jnp.sum(received[:, rows : 2 * rows], axis=0)
    grad_proj = rest * target_row - jnp.sum(weight * received[:, 0:rows], axis=0)
    grad_dot = root_mean * slope
    out_grad = grad_proj / root_mean - hidden_proj * (
        grad_dot / (features * (root_mean * root_mean * root_mean))
    )
    in_proj = jnp.sum(received[:, 2 * rows : 3 * rows], axis=0)
    both = jnp.concatenate([out_grad, in_proj], axis=0).astype(BF16)
    out[...] = jnp.broadcast_to(both[None], out.shape)


def scores_kernel(parts, segments, store_hbm, scores, store, out_grad, in_proj, spread, flat, sem):
    copy = pltpu.make_async_copy(store_hbm, store, sem)
    copy.start()
    chunks, rows = parts.shape[0], parts.shape[1] // 2
    for c in range(chunks):
        both = parts[c].astype(F32)
        here = slice(c * rows, (c + 1) * rows)
        out_grad[here, :] = both[0:rows]
        in_proj[here, :] = both[rows : 2 * rows]
    turned = out_grad[...].T
    tokens = turned.shape[1]
    seqs = flat.shape[0]
    member = (segments[...] == lax.broadcasted_iota(jnp.int32, (seqs, tokens), 0)).astype(F32)
    for p in range(turned.shape[0]):
        spread[p * seqs : (p + 1) * seqs, :] = turned[p : p + 1, :] * member
    grads = dot(spread[...].astype(BF16), in_proj[...].astype(BF16))
    width = grads.shape[1]
    for p in range(turned.shape[0]):
        flat[:, p * width : (p + 1) * width] = grads[p * seqs : (p + 1) * seqs, :]
    copy.wait()
    result = dot(flat[...].astype(BF16), store[...], ((1,), (1,)))
    scores[...] = result[0 : scores.shape[0], :]


def swap(x, size, mask):
    vocab = size["vocab"]
    count = size["dp"] * vocab
    return lax.ppermute(x, AXES, [(i, i ^ mask) for i in range(count)])


def body(size, hidden, inputs, gain, unembed, proj_out, proj_in, targets, segment_ids, store):
    n_dp, n_vocab = size["dp"], size["vocab"]
    devices = n_dp * n_vocab
    tokens, features = targets.shape[0], gain.shape[0]
    per_device = tokens // devices
    rows, width = hidden.shape
    seqs = tokens // 32
    entries = unembed.shape[0]
    projected = proj_out.shape[1]
    gain_row = gain.reshape(1, features)

    def mine(axis):
        return lambda: lax.axis_index(axis)

    if n_dp == 8 and n_vocab == 4 and width % 128 == 0:
        row_block = jnp.concatenate([hidden] + [swap(hidden, size, k) for k in range(1, n_vocab)], axis=0)
        row_offsets = ((rows, lambda k: (lax.axis_index("vocab") ^ k) * width),)
        row_pieces = (row_block,)
        near = {0: row_block}
        for r in (2, 4, 6):
            near[r] = swap(row_block, size, r * n_vocab)
        pieces = dict(near)
        for r in (0, 2, 4, 6):
            pieces[r + 1] = swap(near[r], size, n_vocab)
        layout = tuple(
            tuple(
                (
                    k * rows,
                    rows,
                    lambda r=r: (lax.axis_index("dp") ^ r) * rows,
                    lambda k=k: (lax.axis_index("vocab") ^ k) * width,
                )
                for k in range(n_vocab)
            )
            for r in range(n_dp)
        )
        pieces = [pieces[r] for r in range(n_dp)]
    else:
        row_block = lax.all_gather(hidden, "vocab", axis=1, tiled=True)
        row_offsets = ((rows, lambda k: 0),)
        row_pieces = (row_block,)
        pieces = [lax.all_gather(row_block, "dp", axis=0, tiled=True)]
        layout = (((0, tokens, lambda: 0, lambda: 0),),)

    sds = jax.ShapeDtypeStruct
    weights, in_part, target_column = call(
        early_kernel,
        (
            sds((entries, projected), F32),
            sds((n_vocab, per_device, projected), F32),
            sds((tokens, 128), F32),
        ),
        6,
        name="early",
        us=4.0,
    )(inputs, proj_in, unembed, gain_row, proj_out, targets.reshape(1, tokens))
    aux = call(
        functools.partial(row_kernel, row_offsets),
        sds((n_vocab, per_device, 256), F32),
        len(row_pieces) + 1,
        name="row",
        us=2.0,
    )(*row_pieces, proj_out)
    partial = call(
        functools.partial(logits_kernel, layout),
        sds((devices, 4 * per_device, projected), BF16),
        len(pieces) + 5,
        any_at=(len(pieces),),
        scratch=(
            pltpu.VMEM(unembed.shape, BF16),
            pltpu.VMEM((tokens, features), F32),
            pltpu.VMEM((tokens, features), BF16),
            pltpu.VMEM((tokens, 128), F32),
            pltpu.SemaphoreType.DMA,
        ),
        name="logits",
        us=4.0,
    )(*pieces, unembed, gain_row, target_column, weights, in_part)
    partial = lax.all_to_all(partial, AXES, 0, 0, tiled=True)
    merged, logprob = call(
        functools.partial(merge_kernel, features),
        (sds((devices, 2 * per_device, projected), BF16), sds((1, rows), F32)),
        2,
        name="merge",
    )(partial, aux)
    merged = lax.all_to_all(merged, AXES, 0, 0, tiled=True)
    padded = -(-seqs // 8) * 8
    scores = call(
        scores_kernel,
        sds((seqs, store.shape[0]), F32),
        3,
        any_at=(2,),
        scratch=(
            pltpu.VMEM(store.shape, BF16),
            pltpu.VMEM((tokens, projected), F32),
            pltpu.VMEM((tokens, projected), F32),
            pltpu.VMEM((projected * padded, tokens), F32),
            pltpu.VMEM((padded, store.shape[1]), F32),
            pltpu.SemaphoreType.DMA,
        ),
        name="scores",
    )(merged, segment_ids.reshape(1, tokens), store)
    return scores, logprob.reshape(rows)


def solution(mesh):
    size = dict(mesh.shape)
    in_specs = (
        P("dp", "vocab"),
        P("dp", "vocab"),
        P(),
        P(AXES, None),
        P(),
        P(),
        P(),
        P(),
        P(AXES, None),
    )
    out_specs = (P(None, AXES), P("dp"))
    return jax.shard_map(
        functools.partial(body, size), mesh=mesh, in_specs=in_specs, out_specs=out_specs, check_vma=False
    )
```

```python
import functools

import jax
import jax.numpy as jnp
from jax import lax
from jax.experimental import pallas as pl
from jax.experimental.pallas import tpu as pltpu
from jax.sharding import PartitionSpec as P

EPSILON = 1e-06
AXES = ("dp", "vocab")
F32 = jnp.float32
BF16 = jnp.bfloat16


VMEM = pl.BlockSpec(memory_space=pltpu.VMEM)
ANY = pl.BlockSpec(memory_space=pl.ANY)


def split(x):
    high = x.astype(BF16)
    return high, (x - high.astype(F32)).astype(BF16)


def dot(a, b, dims=((1,), (0,))):
    return lax.dot_general(a, b, (dims, ((), ())), preferred_element_type=F32)


def call(kernel, out_shape, n_in, any_at=(), scratch=(), name=None, us=1.0):
    specs = [ANY if i in any_at else VMEM for i in range(n_in)]
    outs = jax.tree.map(lambda _: VMEM, out_shape)
    return pl.pallas_call(
        kernel,
        out_shape=out_shape,
        in_specs=specs,
        out_specs=outs,
        scratch_shapes=list(scratch),
        name=name,
        cost_estimate=pl.CostEstimate(flops=0, transcendentals=0, bytes_accessed=int(us * 3_000_000)),
        compiler_params=pltpu.CompilerParams(vmem_limit_bytes=32 * 1024 * 1024),
    )


def early_kernel(inputs, proj_in, unembed, gain, proj_out, targets, weights, in_part, target_column):
    scaled_high, scaled_low = split(unembed[...].astype(F32) * gain[...])
    weights[...] = dot(scaled_high, proj_out[...]) + dot(scaled_low, proj_out[...])
    width = inputs.shape[1]
    start = pl.multiple_of(lax.axis_index("vocab") * width, 16)
    part = dot(inputs[...], proj_in[pl.ds(start, width), :])
    chunks, rows, _ = in_part.shape
    for c in range(chunks):
        in_part[c] = part[c * rows : (c + 1) * rows]
    tokens = targets.shape[1]
    target_column[...] = jnp.broadcast_to(targets[...].astype(F32), (128, tokens)).T


def row_kernel(offsets, *refs):
    pieces, proj_out, aux = refs[:-2], refs[-2], refs[-1]
    total, squares, features = 0.0, 0.0, 0
    for piece, (rows, start_of) in zip(pieces, offsets, strict=True):
        for k in range(piece.shape[0] // rows):
            block = piece[k * rows : (k + 1) * rows, :]
            width = block.shape[1]
            start = pl.multiple_of(start_of(k), 16)
            total = total + dot(block, proj_out[pl.ds(start, width), :])
            wide = block.astype(F32)
            squares = squares + jnp.sum(wide * wide, axis=1, keepdims=True)
            features += width
    root_mean = jnp.sqrt(squares / features + EPSILON)
    root_mean = jnp.broadcast_to(root_mean, total.shape)
    chunks, rows, _ = aux.shape
    for c in range(chunks):
        aux[c, :, 0:128] = total[c * rows : (c + 1) * rows]
        aux[c, :, 128:256] = root_mean[c * rows : (c + 1) * rows]


def logits_kernel(layout, *refs):
    n = len(layout)
    pieces = refs[:n]
    unembed_hbm, gain, target_column, weights, in_part, out, unembed, scaled, normed, squares, sem = refs[n:]
    copy = pltpu.make_async_copy(unembed_hbm, unembed, sem)
    copy.start()
    tokens, features = scaled.shape
    squares[...] = jnp.zeros_like(squares)
    for piece, blocks in zip(pieces, layout, strict=True):
        for row, rows, token_at, feature_at in blocks:
            block = piece[row : row + rows, :].astype(F32)
            width = block.shape[1]
            token = pl.multiple_of(token_at(), 16)
            feature = pl.multiple_of(feature_at(), 128)
            partial = jnp.sum(block * block, axis=1, keepdims=True)
            squares[pl.ds(token, rows), :] += jnp.broadcast_to(partial, (rows, 128))
            scaled[pl.ds(token, rows), pl.ds(feature, width)] = block * gain[:, pl.ds(feature, width)]
    inverse = 1.0 / jnp.sqrt(squares[...] / features + EPSILON)
    normed[...] = (scaled[...] * inverse[:, 0:1]).astype(BF16)
    copy.wait()
    logits = dot(normed[...], unembed[...], ((1,), (1,)))
    entries = logits.shape[1]
    place = lax.axis_index("dp") * lax.axis_size("vocab") + lax.axis_index("vocab")
    column = lax.broadcasted_iota(jnp.int32, logits.shape, 1) + place * entries
    onehot = target_column[:, 0:1] == column.astype(F32)
    peak = jnp.max(logits, axis=1, keepdims=True)
    shifted = logits - peak
    other = jnp.where(onehot, 0.0, jnp.exp(shifted))
    total = jnp.sum(other, axis=1, keepdims=True)
    moment = jnp.sum(other * shifted, axis=1, keepdims=True)
    target_logit = jnp.sum(jnp.where(onehot, logits, 0.0), axis=1, keepdims=True)
    w_high, w_low = split(weights[...])
    p_high, p_low = split(other)
    sums = dot(p_high, w_high) + (dot(p_high, w_low) + dot(p_low, w_high))
    hot = onehot.astype(F32).astype(BF16)
    target_row = dot(hot, w_high) + dot(hot, w_low)
    lane = lax.broadcasted_iota(jnp.int32, (tokens, 128), 1)
    which = (lane // 2) % 4
    stats = jnp.where(which < 2, jnp.where(which == 0, peak, total), jnp.where(which == 2, moment, target_logit))
    high = stats.astype(BF16).astype(F32)
    middle = (stats - high).astype(BF16).astype(F32)
    low = stats - high - middle
    piece = (lane // 8) % 4
    stats = jnp.where(piece == 0, high, jnp.where(piece == 1, middle, jnp.where(piece == 2, low, 0.0)))
    chunks, rows = out.shape[0], tokens // out.shape[0]
    own = in_part.shape[0]
    mine = lax.axis_index("dp")
    block = lax.broadcasted_iota(jnp.int32, (rows, 128), 1) // (128 // own)
    for d in range(chunks // own):
        row_stats = stats[d * own * rows : (d * own + 1) * rows]
        for k in range(1, own):
            c = d * own + k
            row_stats = jnp.where(block == k, stats[c * rows : (c + 1) * rows], row_stats)
        for k in range(own):
            c = d * own + k
            here = slice(c * rows, (c + 1) * rows)
            terms = jnp.where(mine == d, in_part[k], 0.0)
            out[c] = jnp.concatenate([sums[here], target_row[here], terms, row_stats], axis=0).astype(BF16)


def merge_kernel(features, parts, aux, out, logprob):
    index, own = lax.axis_index("vocab"), lax.axis_size("vocab")
    hidden_proj = aux[index, :, 0:128]
    root_mean = aux[index, :, 128:256]
    chunks, rows = parts.shape[0], hidden_proj.shape[0]
    received = parts[...].astype(F32)
    stats = received[:, 3 * rows : 4 * rows].reshape(chunks * rows, 128)
    stats = stats + pltpu.roll(stats, 128 - 8, 1) + pltpu.roll(stats, 128 - 16, 1)
    shape = (chunks, rows, 128)
    peak, total = stats.reshape(shape), pltpu.roll(stats, 128 - 2, 1).reshape(shape)
    moment = pltpu.roll(stats, 128 - 4, 1).reshape(shape)
    target_logit = jnp.sum(pltpu.roll(stats, 128 - 6, 1).reshape(shape), axis=0)
    row_peak = jnp.max(peak, axis=0)
    scale = jnp.exp(peak - row_peak[None])
    row_total = jnp.sum(scale * total, axis=0) + jnp.exp(target_logit - row_peak)
    weight = scale / row_total[None]
    rest = jnp.sum(weight * total, axis=0)
    slope = jnp.sum(weight * (total * (target_logit[None] - peak) - moment), axis=0)
    log_of = target_logit - row_peak - jnp.log(row_total)
    group = 128 // own
    lane = lax.broadcasted_iota(jnp.int32, (rows, 128), 1)
    row = lax.broadcasted_iota(jnp.int32, (rows, 128), 0)
    spread = jnp.zeros((rows, 128), F32)
    for k in range(own):
        spread = jnp.where(lane == k * rows + row, log_of[:, k * group : k * group + 1], spread)
    logprob[...] = jnp.sum(spread, axis=0, keepdims=True)[:, 0 : logprob.shape[1]]

    def pick(x):
        at = lax.broadcasted_iota(jnp.int32, x.shape, x.ndim - 1) == index * group
        return jnp.sum(jnp.where(at, x, 0.0), axis=-1, keepdims=True)

    weight, rest, slope = pick(weight), pick(rest), pick(slope)
    target_row = jnp.sum(received[:, rows : 2 * rows], axis=0)
    grad_proj = rest * target_row - jnp.sum(weight * received[:, 0:rows], axis=0)
    grad_dot = root_mean * slope
    out_grad = grad_proj / root_mean - hidden_proj * (
        grad_dot / (features * (root_mean * root_mean * root_mean))
    )
    in_proj = jnp.sum(received[:, 2 * rows : 3 * rows], axis=0)
    both = jnp.concatenate([out_grad, in_proj], axis=0).astype(BF16)
    out[...] = jnp.broadcast_to(both[None], out.shape)


def scores_kernel(parts, segments, store_hbm, scores, store, out_grad, in_proj, spread, flat, sem):
    copy = pltpu.make_async_copy(store_hbm, store, sem)
    copy.start()
    chunks, rows = parts.shape[0], parts.shape[1] // 2
    for c in range(chunks):
        both = parts[c].astype(F32)
        here = slice(c * rows, (c + 1) * rows)
        out_grad[here, :] = both[0:rows]
        in_proj[here, :] = both[rows : 2 * rows]
    turned = out_grad[...].T
    tokens = turned.shape[1]
    seqs = flat.shape[0]
    member = (segments[...] == lax.broadcasted_iota(jnp.int32, (seqs, tokens), 0)).astype(F32)
    for p in range(turned.shape[0]):
        spread[p * seqs : (p + 1) * seqs, :] = turned[p : p + 1, :] * member
    grads = dot(spread[...].astype(BF16), in_proj[...].astype(BF16))
    width = grads.shape[1]
    for p in range(turned.shape[0]):
        flat[:, p * width : (p + 1) * width] = grads[p * seqs : (p + 1) * seqs, :]
    copy.wait()
    result = dot(flat[...].astype(BF16), store[...], ((1,), (1,)))
    scores[...] = result[0 : scores.shape[0], :]


def swap(x, size, mask):
    vocab = size["vocab"]
    count = size["dp"] * vocab
    return lax.ppermute(x, AXES, [(i, i ^ mask) for i in range(count)])


def body(size, hidden, inputs, gain, unembed, proj_out, proj_in, targets, segment_ids, store):
    n_dp, n_vocab = size["dp"], size["vocab"]
    devices = n_dp * n_vocab
    tokens, features = targets.shape[0], gain.shape[0]
    per_device = tokens // devices
    rows, width = hidden.shape
    seqs = tokens // 32
    entries = unembed.shape[0]
    projected = proj_out.shape[1]
    gain_row = gain.reshape(1, features)

    sds = jax.ShapeDtypeStruct

    def side_work(inputs, row_pieces, row_offsets):
        weights, in_part, target_column = call(
            early_kernel,
            (
                sds((entries, projected), F32),
                sds((n_vocab, per_device, projected), F32),
                sds((tokens, 128), F32),
            ),
            6,
            name="early",
            us=4.0,
        )(inputs, proj_in, unembed, gain_row, proj_out, targets.reshape(1, tokens))
        aux = call(
            functools.partial(row_kernel, row_offsets),
            sds((n_vocab, per_device, 256), F32),
            len(row_pieces) + 1,
            name="row",
            us=2.0,
        )(*row_pieces, proj_out)
        return weights, in_part, target_column, aux

    def mine(axis):
        return lambda: lax.axis_index(axis)

    if n_dp == 8 and n_vocab == 4 and width % 128 == 0:
        row_block = jnp.concatenate([hidden] + [swap(hidden, size, k) for k in range(1, n_vocab)], axis=0)
        row_offsets = ((rows, lambda k: (lax.axis_index("vocab") ^ k) * width),)
        row_pieces = (row_block,)
        near = {0: row_block}
        for r in (2, 4, 6):
            near[r] = swap(row_block, size, r * n_vocab)
        early_inputs, _ = lax.optimization_barrier((inputs, row_block))
        side = side_work(early_inputs, row_pieces, row_offsets)
        near[2], near[4], near[6], side = lax.optimization_barrier((near[2], near[4], near[6], side))
        pieces = dict(near)
        for r in (0, 2, 4, 6):
            pieces[r + 1] = swap(near[r], size, n_vocab)
        layout = tuple(
            tuple(
                (
                    k * rows,
                    rows,
                    lambda r=r: (lax.axis_index("dp") ^ r) * rows,
                    lambda k=k: (lax.axis_index("vocab") ^ k) * width,
                )
                for k in range(n_vocab)
            )
            for r in range(n_dp)
        )
        pieces = [pieces[r] for r in range(n_dp)]
    else:
        row_block = lax.all_gather(hidden, "vocab", axis=1, tiled=True)
        row_offsets = ((rows, lambda k: 0),)
        row_pieces = (row_block,)
        pieces = [lax.all_gather(row_block, "dp", axis=0, tiled=True)]
        layout = (((0, tokens, lambda: 0, lambda: 0),),)
        side = side_work(inputs, row_pieces, row_offsets)
    weights, in_part, target_column, aux = side

    partial = call(
        functools.partial(logits_kernel, layout),
        sds((devices, 4 * per_device, projected), BF16),
        len(pieces) + 5,
        any_at=(len(pieces),),
        scratch=(
            pltpu.VMEM(unembed.shape, BF16),
            pltpu.VMEM((tokens, features), F32),
            pltpu.VMEM((tokens, features), BF16),
            pltpu.VMEM((tokens, 128), F32),
            pltpu.SemaphoreType.DMA,
        ),
        name="logits",
        us=4.0,
    )(*pieces, unembed, gain_row, target_column, weights, in_part)
    partial = lax.all_to_all(partial, AXES, 0, 0, tiled=True)
    merged, logprob = call(
        functools.partial(merge_kernel, features),
        (sds((devices, 2 * per_device, projected), BF16), sds((1, rows), F32)),
        2,
        name="merge",
    )(partial, aux)
    merged = lax.all_to_all(merged, AXES, 0, 0, tiled=True)
    padded = -(-seqs // 8) * 8
    scores = call(
        scores_kernel,
        sds((seqs, store.shape[0]), F32),
        3,
        any_at=(2,),
        scratch=(
            pltpu.VMEM(store.shape, BF16),
            pltpu.VMEM((tokens, projected), F32),
            pltpu.VMEM((tokens, projected), F32),
            pltpu.VMEM((projected * padded, tokens), F32),
            pltpu.VMEM((padded, store.shape[1]), F32),
            pltpu.SemaphoreType.DMA,
        ),
        name="scores",
    )(merged, segment_ids.reshape(1, tokens), store)
    return scores, logprob.reshape(rows)


def solution(mesh):
    size = dict(mesh.shape)
    in_specs = (
        P("dp", "vocab"),
        P("dp", "vocab"),
        P(),
        P(AXES, None),
        P(),
        P(),
        P(),
        P(),
        P(AXES, None),
    )
    out_specs = (P(None, AXES), P("dp"))
    return jax.shard_map(
        functools.partial(body, size), mesh=mesh, in_specs=in_specs, out_specs=out_specs, check_vma=False
    )
```

```python
import functools

import jax
import jax.numpy as jnp
from jax import lax
from jax.experimental import pallas as pl
from jax.experimental.pallas import tpu as pltpu
from jax.sharding import PartitionSpec as P


EPSILON = 1e-06
AXES = ("dp", "vocab")
F32 = jnp.float32
BF16 = jnp.bfloat16


VMEM = pl.BlockSpec(memory_space=pltpu.VMEM)
HBM = pl.BlockSpec(memory_space=pltpu.HBM)


def split(x):
    high = x.astype(BF16)
    return high, (x - high.astype(F32)).astype(BF16)


def dot(a, b, dims=((1,), (0,))):
    return lax.dot_general(a, b, (dims, ((), ())), preferred_element_type=F32)


def call(kernel, out_shape, n_in, hbm_at=(), scratch=(), us=1.0):
    specs = [HBM if i in hbm_at else VMEM for i in range(n_in)]
    outs = jax.tree.map(lambda _: VMEM, out_shape)
    run = pl.pallas_call(
        kernel,
        out_shape=out_shape,
        in_specs=specs,
        out_specs=outs,
        scratch_shapes=list(scratch),
        cost_estimate=pl.CostEstimate(flops=0, transcendentals=0, bytes_accessed=int(us * 3_000_000)),
        compiler_params=pltpu.CompilerParams(vmem_limit_bytes=32 * 1024 * 1024),
    )

    def placed(*args):
        return run(
            *[pltpu.with_memory_space_constraint(x, pltpu.HBM) if i in hbm_at else x for i, x in enumerate(args)]
        )

    return placed


def stage_kernel(hidden_hbm, gain_hbm, hidden, gain, sems):
    copies = [
        pltpu.make_async_copy(hidden_hbm, hidden, sems.at[0]),
        pltpu.make_async_copy(gain_hbm, gain, sems.at[1]),
    ]
    for copy in copies:
        copy.start()
    for copy in copies:
        copy.wait()


def norm_kernel(offsets, *refs):
    pieces, gain, normed, root_mean = refs[:-3], refs[-3], refs[-2], refs[-1]
    squares, features = 0.0, 0
    for piece in pieces:
        wide = piece[...].astype(F32)
        squares = squares + jnp.sum(wide * wide, axis=1, keepdims=True)
        features += wide.shape[1]
    root = jnp.sqrt(squares / features + EPSILON)
    inverse = 1.0 / root
    for piece, offset in zip(pieces, offsets, strict=True):
        width = piece.shape[1]
        here = pl.ds(pl.multiple_of(offset(), 128), width)
        normed[:, here] = (piece[...].astype(F32) * gain[:, here] * inverse).astype(BF16)
    wide_root = jnp.broadcast_to(root, (root.shape[0], 128))
    chunks, rows, _ = root_mean.shape
    for c in range(chunks):
        root_mean[c] = wide_root[c * rows : (c + 1) * rows]


def side_kernel(offsets, *refs):
    n = len(offsets)
    pieces = refs[:n]
    sources, gain = refs[n : n + 5], refs[n + 5]
    weights, in_part, hidden_proj, target_column = refs[n + 6 : n + 10]
    buffers, sems = refs[n + 10 : n + 15], refs[n + 15]
    copies = [
        pltpu.make_async_copy(source, buffer, sems.at[i])
        for i, (source, buffer) in enumerate(zip(sources, buffers, strict=True))
    ]
    for copy in copies:
        copy.start()
    proj_out, unembed, proj_in, inputs, targets = buffers
    copies[0].wait()
    total = 0.0
    for piece, offset in zip(pieces, offsets, strict=True):
        width = piece.shape[1]
        total = total + dot(piece[...], proj_out[pl.ds(pl.multiple_of(offset(), 16), width), :])
    copies[1].wait()
    scaled_high, scaled_low = split(unembed[...].astype(F32) * gain[...])
    weights[...] = dot(scaled_high, proj_out[...]) + dot(scaled_low, proj_out[...])
    for copy in copies[2:]:
        copy.wait()
    tokens = targets.shape[1]
    target_column[...] = jnp.broadcast_to(targets[...].astype(F32), (128, tokens)).T
    width = inputs.shape[1]
    start = pl.multiple_of(lax.axis_index("vocab") * width, 16)
    part = dot(inputs[...], proj_in[pl.ds(start, width), :])
    chunks, rows, _ = in_part.shape
    for c in range(chunks):
        in_part[c] = part[c * rows : (c + 1) * rows]
        hidden_proj[c] = total[c * rows : (c + 1) * rows]


def logits_kernel(order, *refs):
    n = len(order)
    pieces = refs[:n]
    unembed, target_column, weights, in_part, out, placed = refs[n:]
    rows = pieces[0].shape[0]
    relative = dot(jnp.concatenate([piece[...] for piece in pieces], axis=0), unembed[...], ((1,), (1,)))
    for k, token_at in enumerate(order):
        placed[pl.ds(pl.multiple_of(token_at(), 16), rows), :] = relative[k * rows : (k + 1) * rows]
    logits = placed[...]
    tokens = logits.shape[0]
    entries = logits.shape[1]
    place = lax.axis_index("dp") * lax.axis_size("vocab") + lax.axis_index("vocab")
    column = lax.broadcasted_iota(jnp.int32, logits.shape, 1) + place * entries
    onehot = target_column[:, 0:1] == column.astype(F32)
    peak = jnp.max(logits, axis=1, keepdims=True)
    shifted = logits - peak
    other = jnp.where(onehot, 0.0, jnp.exp(shifted))
    total = jnp.sum(other, axis=1, keepdims=True)
    moment = jnp.sum(other * shifted, axis=1, keepdims=True)
    target_logit = jnp.sum(jnp.where(onehot, logits, 0.0), axis=1, keepdims=True)
    w_high, w_low = split(weights[...])
    p_high, p_low = split(other)
    sums = dot(p_high, w_high) + (dot(p_high, w_low) + dot(p_low, w_high))
    hot = onehot.astype(F32).astype(BF16)
    target_row = dot(hot, w_high) + dot(hot, w_low)
    lane = lax.broadcasted_iota(jnp.int32, (tokens, 128), 1)
    which = (lane // 2) % 4
    stats = jnp.where(which < 2, jnp.where(which == 0, peak, total), jnp.where(which == 2, moment, target_logit))
    high = stats.astype(BF16).astype(F32)
    middle = (stats - high).astype(BF16).astype(F32)
    low = stats - high - middle
    piece = (lane // 8) % 4
    stats = jnp.where(piece == 0, high, jnp.where(piece == 1, middle, jnp.where(piece == 2, low, 0.0)))
    chunks, rows = out.shape[0], tokens // out.shape[0]
    own = in_part.shape[0]
    mine = lax.axis_index("dp")
    block = lax.broadcasted_iota(jnp.int32, (rows, 128), 1) // (128 // own)
    for d in range(chunks // own):
        row_stats = stats[d * own * rows : (d * own + 1) * rows]
        for k in range(1, own):
            c = d * own + k
            row_stats = jnp.where(block == k, stats[c * rows : (c + 1) * rows], row_stats)
        for k in range(own):
            c = d * own + k
            here = slice(c * rows, (c + 1) * rows)
            terms = jnp.where(mine == d, in_part[k], 0.0)
            out[c] = jnp.concatenate([sums[here], target_row[here], terms, row_stats], axis=0).astype(BF16)


def merge_kernel(features, parts, hidden_projs, root_means, out, logprob):
    index, own = lax.axis_index("vocab"), lax.axis_size("vocab")
    hidden_proj = hidden_projs[index]
    root_mean = root_means[index]
    chunks, rows = parts.shape[0], hidden_proj.shape[0]
    received = parts[...].astype(F32)
    stats = received[:, 3 * rows : 4 * rows].reshape(chunks * rows, 128)
    stats = stats + pltpu.roll(stats, 128 - 8, 1) + pltpu.roll(stats, 128 - 16, 1)
    shape = (chunks, rows, 128)
    peak, total = stats.reshape(shape), pltpu.roll(stats, 128 - 2, 1).reshape(shape)
    moment = pltpu.roll(stats, 128 - 4, 1).reshape(shape)
    target_logit = jnp.sum(pltpu.roll(stats, 128 - 6, 1).reshape(shape), axis=0)
    row_peak = jnp.max(peak, axis=0)
    scale = jnp.exp(peak - row_peak[None])
    row_total = jnp.sum(scale * total, axis=0) + jnp.exp(target_logit - row_peak)
    weight = scale / row_total[None]
    rest = jnp.sum(weight * total, axis=0)
    slope = jnp.sum(weight * (total * (target_logit[None] - peak) - moment), axis=0)
    log_of = target_logit - row_peak - jnp.log(row_total)
    group = 128 // own
    lane = lax.broadcasted_iota(jnp.int32, (rows, 128), 1)
    row = lax.broadcasted_iota(jnp.int32, (rows, 128), 0)
    spread = jnp.zeros((rows, 128), F32)
    for k in range(own):
        spread = jnp.where(lane == k * rows + row, log_of[:, k * group : k * group + 1], spread)
    logprob[...] = jnp.sum(spread, axis=0, keepdims=True)[:, 0 : logprob.shape[1]]

    def pick(x):
        at = lax.broadcasted_iota(jnp.int32, x.shape, x.ndim - 1) == index * group
        return jnp.sum(jnp.where(at, x, 0.0), axis=-1, keepdims=True)

    weight, rest, slope = pick(weight), pick(rest), pick(slope)
    target_row = jnp.sum(received[:, rows : 2 * rows], axis=0)
    grad_proj = rest * target_row - jnp.sum(weight * received[:, 0:rows], axis=0)
    grad_dot = root_mean * slope
    out_grad = grad_proj / root_mean - hidden_proj * (
        grad_dot / (features * (root_mean * root_mean * root_mean))
    )
    in_proj = jnp.sum(received[:, 2 * rows : 3 * rows], axis=0)
    both = jnp.concatenate([out_grad, in_proj], axis=0).astype(BF16)
    out[...] = jnp.broadcast_to(both[None], out.shape)


def scores_kernel(parts, segments, store, scores, out_grad, in_proj, spread, flat):
    chunks, rows = parts.shape[0], parts.shape[1] // 2
    for c in range(chunks):
        both = parts[c].astype(F32)
        here = slice(c * rows, (c + 1) * rows)
        out_grad[here, :] = both[0:rows]
        in_proj[here, :] = both[rows : 2 * rows]
    turned = out_grad[...].T
    tokens = turned.shape[1]
    seqs = flat.shape[0]
    member = (segments[...] == lax.broadcasted_iota(jnp.int32, (seqs, tokens), 0)).astype(F32)
    for p in range(turned.shape[0]):
        spread[p * seqs : (p + 1) * seqs, :] = turned[p : p + 1, :] * member
    grads = dot(spread[...].astype(BF16), in_proj[...].astype(BF16))
    width = grads.shape[1]
    for p in range(turned.shape[0]):
        flat[:, p * width : (p + 1) * width] = grads[p * seqs : (p + 1) * seqs, :]
    result = dot(flat[...].astype(BF16), store[...], ((1,), (1,)))
    scores[...] = result[0 : scores.shape[0], :]


def swap(x, size, mask):
    vocab = size["vocab"]
    count = size["dp"] * vocab
    return lax.ppermute(x, AXES, [(i, i ^ mask) for i in range(count)])


def body(size, *args):
    return steps(size, *args)


def steps(size, hidden, inputs, gain, unembed, proj_out, proj_in, targets, segment_ids, store):
    n_dp, n_vocab = size["dp"], size["vocab"]
    devices = n_dp * n_vocab
    tokens, features = targets.shape[0], gain.shape[0]
    per_device = tokens // devices
    rows, width = hidden.shape
    seqs = tokens // 32
    entries = unembed.shape[0]
    projected = proj_out.shape[1]
    gain_row = gain.reshape(1, features)

    sds = jax.ShapeDtypeStruct
    row_shape = sds((n_vocab, per_device, projected), F32)

    def norm(row_pieces, offsets, gain_row):
        return call(
            functools.partial(norm_kernel, offsets), (sds((rows, features), BF16), row_shape), len(row_pieces) + 1
        )(*row_pieces, gain_row)

    def side_work(row_pieces, offsets, gain_row):
        n = len(row_pieces)
        sources = (proj_out, unembed, proj_in, inputs, targets.reshape(1, tokens))
        return call(
            functools.partial(side_kernel, offsets),
            (sds((entries, projected), F32), row_shape, row_shape, sds((tokens, 128), F32)),
            n + 6,
            hbm_at=range(n, n + 5),
            scratch=[pltpu.VMEM(x.shape, x.dtype) for x in sources] + [pltpu.SemaphoreType.DMA((5,))],
            us=4.0,
        )(*row_pieces, *sources, gain_row)

    if n_dp == 8 and n_vocab == 4 and width % 128 == 0:
        row_pieces = [swap(hidden, size, k) for k in (2, 3, 1)]
        staged, gain_row = call(
            stage_kernel,
            (sds(hidden.shape, BF16), sds(gain_row.shape, F32)),
            2,
            hbm_at=(0, 1),
            scratch=[pltpu.SemaphoreType.DMA((2,))],
        )(hidden, gain_row)
        row_pieces = [staged] + row_pieces
        offsets = [lambda k=k: (lax.axis_index("vocab") ^ k) * width for k in (0, 2, 3, 1)]
        normed, root_mean = norm(row_pieces, offsets, gain_row)
        near = {0: normed}
        for r in (6, 2, 4):
            near[r] = swap(normed, size, r * n_vocab)
        *row_pieces, _ = lax.optimization_barrier((*row_pieces, normed))
        side = side_work(row_pieces, offsets, gain_row)
        near[2], near[4], near[6], side = lax.optimization_barrier((near[2], near[4], near[6], side))
        pieces = dict(near)
        for r in (0, 6, 2, 4):
            pieces[r + 1] = swap(near[r], size, n_vocab)
        pieces = [pieces[r] for r in range(n_dp)]
        order = [lambda r=r: (lax.axis_index("dp") ^ r) * rows for r in range(n_dp)]
    else:
        row_pieces = [lax.all_gather(hidden, "vocab", axis=1, tiled=True)]
        offsets = [lambda: 0]
        normed, root_mean = norm(row_pieces, offsets, gain_row)
        side = side_work(row_pieces, offsets, gain_row)
        pieces = [lax.all_gather(normed, "dp", axis=0, tiled=True)]
        order = [lambda: 0]
    weights, in_part, hidden_proj, target_column = side
    partial = call(
        functools.partial(logits_kernel, order),
        sds((devices, 4 * per_device, projected), BF16),
        len(pieces) + 4,
        scratch=[pltpu.VMEM((tokens, entries), F32)],
        us=2.0,
    )(*pieces, unembed, target_column, weights, in_part)
    partial = lax.all_to_all(partial, AXES, 0, 0, tiled=True)
    merged, logprob = call(
        functools.partial(merge_kernel, features),
        (sds((devices, 2 * per_device, projected), BF16), sds((1, rows), F32)),
        3,
    )(partial, hidden_proj, root_mean)
    merged = lax.all_to_all(merged, AXES, 0, 0, tiled=True)
    padded = -(-seqs // 8) * 8
    scores = call(
        scores_kernel,
        sds((seqs, store.shape[0]), F32),
        3,
        scratch=(
            pltpu.VMEM((tokens, projected), F32),
            pltpu.VMEM((tokens, projected), F32),
            pltpu.VMEM((projected * padded, tokens), F32),
            pltpu.VMEM((padded, store.shape[1]), F32),
        ),
    )(merged, segment_ids.reshape(1, tokens), store)
    return scores, logprob.reshape(rows)


def solution(mesh):
    size = dict(mesh.shape)
    in_specs = (
        P("dp", "vocab"),
        P("dp", "vocab"),
        P(),
        P(AXES, None),
        P(),
        P(),
        P(),
        P(),
        P(AXES, None),
    )
    out_specs = (P(None, AXES), P("dp"))
    return jax.shard_map(
        functools.partial(body, size), mesh=mesh, in_specs=in_specs, out_specs=out_specs, check_vma=False
    )
```

```python
import functools

import jax
import jax.numpy as jnp
from jax import lax
from jax.experimental import pallas as pl
from jax.experimental.pallas import tpu as pltpu
from jax.sharding import PartitionSpec as P


EPSILON = 1e-06
AXES = ("dp", "vocab")
F32 = jnp.float32
BF16 = jnp.bfloat16


VMEM = pl.BlockSpec(memory_space=pltpu.VMEM)
HBM = pl.BlockSpec(memory_space=pltpu.HBM)


def split(x):
    high = x.astype(BF16)
    return high, (x - high.astype(F32)).astype(BF16)


def dot(a, b, dims=((1,), (0,))):
    return lax.dot_general(a, b, (dims, ((), ())), preferred_element_type=F32)


def call(kernel, out_shape, n_in, hbm_at=(), scratch=(), us=1.0):
    specs = [HBM if i in hbm_at else VMEM for i in range(n_in)]
    outs = jax.tree.map(lambda _: VMEM, out_shape)
    run = pl.pallas_call(
        kernel,
        out_shape=out_shape,
        in_specs=specs,
        out_specs=outs,
        scratch_shapes=list(scratch),
        cost_estimate=pl.CostEstimate(flops=0, transcendentals=0, bytes_accessed=int(us * 3_000_000)),
        compiler_params=pltpu.CompilerParams(vmem_limit_bytes=32 * 1024 * 1024),
    )

    def placed(*args):
        return run(
            *[pltpu.with_memory_space_constraint(x, pltpu.HBM) if i in hbm_at else x for i, x in enumerate(args)]
        )

    return placed


def stage_kernel(hidden_hbm, gain_hbm, hidden, gain, sems):
    copies = [
        pltpu.make_async_copy(hidden_hbm, hidden, sems.at[0]),
        pltpu.make_async_copy(gain_hbm, gain, sems.at[1]),
    ]
    for copy in copies:
        copy.start()
    for copy in copies:
        copy.wait()


def norm_kernel(offsets, *refs):
    pieces, gain, normed, root_mean = refs[:-3], refs[-3], refs[-2], refs[-1]
    squares, features = 0.0, 0
    for piece in pieces:
        wide = piece[...].astype(F32)
        squares = squares + jnp.sum(wide * wide, axis=1, keepdims=True)
        features += wide.shape[1]
    root = jnp.sqrt(squares / features + EPSILON)
    inverse = 1.0 / root
    for piece, offset in zip(pieces, offsets, strict=True):
        width = piece.shape[1]
        here = pl.ds(pl.multiple_of(offset(), 128), width)
        normed[:, here] = (piece[...].astype(F32) * gain[:, here] * inverse).astype(BF16)
    wide_root = jnp.broadcast_to(root, (root.shape[0], 128))
    chunks, rows, _ = root_mean.shape
    for c in range(chunks):
        root_mean[c] = wide_root[c * rows : (c + 1) * rows]


def side_kernel(offsets, others, *refs):
    n = len(offsets)
    pieces, other_unembeds, refs = refs[:n], refs[n : n + others], refs[n + others :]
    sources, gain = refs[:5], refs[5]
    weights, in_part, hidden_proj, target_column = refs[6:10]
    buffers, sems = refs[10:15], refs[15]
    copies = [
        pltpu.make_async_copy(source, buffer, sems.at[i])
        for i, (source, buffer) in enumerate(zip(sources, buffers, strict=True))
    ]
    for copy in copies:
        copy.start()
    proj_out, unembed, proj_in, inputs, targets = buffers
    copies[0].wait()
    total = 0.0
    for piece, offset in zip(pieces, offsets, strict=True):
        width = piece.shape[1]
        total = total + dot(piece[...], proj_out[pl.ds(pl.multiple_of(offset(), 16), width), :])
    copies[1].wait()
    for u, rows_of in enumerate((unembed, *other_unembeds)):
        scaled_high, scaled_low = split(rows_of[...].astype(F32) * gain[...])
        weights[u] = dot(scaled_high, proj_out[...]) + dot(scaled_low, proj_out[...])
    for copy in copies[2:]:
        copy.wait()
    tokens = targets.shape[1]
    target_column[...] = jnp.broadcast_to(targets[...].astype(F32), (128, tokens)).T
    width = inputs.shape[1]
    start = pl.multiple_of(lax.axis_index("vocab") * width, 16)
    part = dot(inputs[...], proj_in[pl.ds(start, width), :])
    chunks, rows, _ = in_part.shape
    for c in range(chunks):
        in_part[c] = part[c * rows : (c + 1) * rows]
        hidden_proj[c] = total[c * rows : (c + 1) * rows]


def logits_kernel(order, twin, *refs):
    n = len(order)
    pieces, unembeds = refs[:n], refs[n : n + twin]
    target_column, weights, in_part, out, placed, placed_target = refs[n + twin :]
    rows = pieces[0].shape[0]
    normed = jnp.concatenate([piece[...] for piece in pieces], axis=0)
    entries = unembeds[0].shape[0]
    mine, own = lax.axis_index("dp"), lax.axis_size("vocab")
    starts = [(pl.multiple_of(local(), 16), pl.multiple_of(whole(), 16)) for local, whole in order]
    for local, whole in starts:
        placed_target[pl.ds(local, rows), :] = target_column[pl.ds(whole, rows), :]
    logits, onehot = [], []
    for u, unembed in enumerate(unembeds):
        relative = dot(normed, unembed[...], ((1,), (1,)))
        for k, (local, _) in enumerate(starts):
            placed[u, pl.ds(local, rows), :] = relative[k * rows : (k + 1) * rows]
        logits.append(placed[u])
        place = (mine ^ u) * own + lax.axis_index("vocab")
        column = lax.broadcasted_iota(jnp.int32, relative.shape, 1) + place * entries
        onehot.append(placed_target[:, 0:1] == column.astype(F32))
    tokens = logits[0].shape[0]
    peak = functools.reduce(jnp.maximum, [jnp.max(x, axis=1, keepdims=True) for x in logits])
    total = moment = target_logit = sums = target_row = 0.0
    for u in range(twin):
        shifted = logits[u] - peak
        other = jnp.where(onehot[u], 0.0, jnp.exp(shifted))
        total = total + jnp.sum(other, axis=1, keepdims=True)
        moment = moment + jnp.sum(other * shifted, axis=1, keepdims=True)
        target_logit = target_logit + jnp.sum(jnp.where(onehot[u], logits[u], 0.0), axis=1, keepdims=True)
        w_high, w_low = split(weights[u])
        p_high, p_low = split(other)
        sums = sums + (dot(p_high, w_high) + (dot(p_high, w_low) + dot(p_low, w_high)))
        hot = onehot[u].astype(F32).astype(BF16)
        target_row = target_row + (dot(hot, w_high) + dot(hot, w_low))
    lane = lax.broadcasted_iota(jnp.int32, (tokens, 128), 1)
    which = (lane // 2) % 4
    stats = jnp.where(which < 2, jnp.where(which == 0, peak, total), jnp.where(which == 2, moment, target_logit))
    high = stats.astype(BF16).astype(F32)
    middle = (stats - high).astype(BF16).astype(F32)
    low = stats - high - middle
    piece = (lane // 8) % 4
    stats = jnp.where(piece == 0, high, jnp.where(piece == 1, middle, jnp.where(piece == 2, low, 0.0)))
    chunks = out.shape[0]
    rows = tokens * twin // chunks
    block = lax.broadcasted_iota(jnp.int32, (rows, 128), 1) // (128 // own)
    for d in range(chunks // own):
        first = d // twin * own
        row_stats = stats[first * rows : (first + 1) * rows]
        for k in range(1, own):
            row_stats = jnp.where(block == k, stats[(first + k) * rows : (first + k + 1) * rows], row_stats)
        for k in range(own):
            here = slice((first + k) * rows, (first + k + 1) * rows)
            terms = jnp.where(mine == d, in_part[k], 0.0)
            packed = jnp.concatenate([sums[here], target_row[here], terms, row_stats], axis=0)
            out[d * own + k] = packed.astype(BF16)


def merge_kernel(features, parts, hidden_projs, root_means, out, logprob):
    index, own = lax.axis_index("vocab"), lax.axis_size("vocab")
    hidden_proj = hidden_projs[index]
    root_mean = root_means[index]
    rows = hidden_proj.shape[0]
    chunks = parts.shape[0] * own
    received = parts[:, lax.axis_index("dp") % parts.shape[1]]
    received = received.reshape(chunks, *received.shape[2:]).astype(F32)
    stats = received[:, 3 * rows : 4 * rows].reshape(chunks * rows, 128)
    stats = stats + pltpu.roll(stats, 128 - 8, 1) + pltpu.roll(stats, 128 - 16, 1)
    shape = (chunks, rows, 128)
    peak, total = stats.reshape(shape), pltpu.roll(stats, 128 - 2, 1).reshape(shape)
    moment = pltpu.roll(stats, 128 - 4, 1).reshape(shape)
    target_logit = jnp.sum(pltpu.roll(stats, 128 - 6, 1).reshape(shape), axis=0)
    row_peak = jnp.max(peak, axis=0)
    scale = jnp.exp(peak - row_peak[None])
    row_total = jnp.sum(scale * total, axis=0) + jnp.exp(target_logit - row_peak)
    weight = scale / row_total[None]
    rest = jnp.sum(weight * total, axis=0)
    slope = jnp.sum(weight * (total * (target_logit[None] - peak) - moment), axis=0)
    log_of = target_logit - row_peak - jnp.log(row_total)
    group = 128 // own
    lane = lax.broadcasted_iota(jnp.int32, (rows, 128), 1)
    row = lax.broadcasted_iota(jnp.int32, (rows, 128), 0)
    spread = jnp.zeros((rows, 128), F32)
    for k in range(own):
        spread = jnp.where(lane == k * rows + row, log_of[:, k * group : k * group + 1], spread)
    logprob[...] = jnp.sum(spread, axis=0, keepdims=True)[:, 0 : logprob.shape[1]]

    def pick(x):
        at = lax.broadcasted_iota(jnp.int32, x.shape, x.ndim - 1) == index * group
        return jnp.sum(jnp.where(at, x, 0.0), axis=-1, keepdims=True)

    weight, rest, slope = pick(weight), pick(rest), pick(slope)
    target_row = jnp.sum(received[:, rows : 2 * rows], axis=0)
    grad_proj = rest * target_row - jnp.sum(weight * received[:, 0:rows], axis=0)
    grad_dot = root_mean * slope
    out_grad = grad_proj / root_mean - hidden_proj * (
        grad_dot / (features * (root_mean * root_mean * root_mean))
    )
    in_proj = jnp.sum(received[:, 2 * rows : 3 * rows], axis=0)
    both = jnp.concatenate([out_grad, in_proj], axis=0).astype(BF16)
    out[...] = jnp.broadcast_to(both[None], out.shape)


def scores_kernel(parts, segments, store, scores, out_grad, in_proj, spread, flat):
    chunks, rows = parts.shape[0], parts.shape[1] // 2
    for c in range(chunks):
        both = parts[c].astype(F32)
        here = slice(c * rows, (c + 1) * rows)
        out_grad[here, :] = both[0:rows]
        in_proj[here, :] = both[rows : 2 * rows]
    turned = out_grad[...].T
    tokens = turned.shape[1]
    seqs = flat.shape[0]
    member = (segments[...] == lax.broadcasted_iota(jnp.int32, (seqs, tokens), 0)).astype(F32)
    for p in range(turned.shape[0]):
        spread[p * seqs : (p + 1) * seqs, :] = turned[p : p + 1, :] * member
    grads = dot(spread[...].astype(BF16), in_proj[...].astype(BF16))
    width = grads.shape[1]
    for p in range(turned.shape[0]):
        flat[:, p * width : (p + 1) * width] = grads[p * seqs : (p + 1) * seqs, :]
    result = dot(flat[...].astype(BF16), store[...], ((1,), (1,)))
    scores[...] = result[0 : scores.shape[0], :]


def swap(x, size, mask):
    vocab = size["vocab"]
    count = size["dp"] * vocab
    return lax.ppermute(x, AXES, [(i, i ^ mask) for i in range(count)])


def body(size, *args):
    return steps(size, *args)


def steps(size, hidden, inputs, gain, unembed, proj_out, proj_in, targets, segment_ids, store):
    n_dp, n_vocab = size["dp"], size["vocab"]
    devices = n_dp * n_vocab
    tokens, features = targets.shape[0], gain.shape[0]
    per_device = tokens // devices
    rows, width = hidden.shape
    seqs = tokens // 32
    entries = unembed.shape[0]
    projected = proj_out.shape[1]
    gain_row = gain.reshape(1, features)

    sds = jax.ShapeDtypeStruct
    fast = n_dp == 8 and n_vocab == 4 and width % 128 == 0
    twin = 2 if fast else 1
    row_shape = sds((n_vocab, per_device, projected), F32)

    def norm(row_pieces, offsets, gain_row):
        return call(
            functools.partial(norm_kernel, offsets), (sds((rows, features), BF16), row_shape), len(row_pieces) + 1
        )(*row_pieces, gain_row)

    def side_work(row_pieces, offsets, others, gain_row):
        n = len(row_pieces)
        sources = (proj_out, unembed, proj_in, inputs, targets.reshape(1, tokens))
        n += len(others)
        return call(
            functools.partial(side_kernel, offsets, len(others)),
            (sds((twin, entries, projected), F32), row_shape, row_shape, sds((tokens, 128), F32)),
            n + 6,
            hbm_at=range(n, n + 5),
            scratch=[pltpu.VMEM(x.shape, x.dtype) for x in sources] + [pltpu.SemaphoreType.DMA((5,))],
            us=4.0,
        )(*row_pieces, *others, *sources, gain_row)

    if fast:
        row_pieces = [swap(hidden, size, k) for k in (2, 3, 1)]
        others = [swap(unembed, size, n_vocab)]
        staged, gain_row = call(
            stage_kernel,
            (sds(hidden.shape, BF16), sds(gain_row.shape, F32)),
            2,
            hbm_at=(0, 1),
            scratch=[pltpu.SemaphoreType.DMA((2,))],
        )(hidden, gain_row)
        row_pieces = [staged] + row_pieces
        offsets = [lambda k=k: (lax.axis_index("vocab") ^ k) * width for k in (0, 2, 3, 1)]
        normed, root_mean = norm(row_pieces, offsets, gain_row)
        *row_pieces, _ = lax.optimization_barrier((*row_pieces, normed))
        side = side_work(row_pieces, offsets, others, gain_row)
        masks = (0, 6, 4, 2)
        pieces = [normed] + [swap(normed, size, r * n_vocab) for r in masks[1:]]
        order = [
            (
                lambda r=r: (lax.axis_index("dp") ^ r) // 2 * rows,
                lambda r=r: (lax.axis_index("dp") ^ r) * rows,
            )
            for r in masks
        ]
    else:
        row_pieces = [lax.all_gather(hidden, "vocab", axis=1, tiled=True)]
        offsets, others = [lambda: 0], []
        normed, root_mean = norm(row_pieces, offsets, gain_row)
        side = side_work(row_pieces, offsets, others, gain_row)
        pieces = [lax.all_gather(normed, "dp", axis=0, tiled=True)]
        order = [(lambda: 0, lambda: 0)]
    weights, in_part, hidden_proj, target_column = side
    partial = call(
        functools.partial(logits_kernel, order, twin),
        sds((devices, 4 * per_device, projected), BF16),
        len(pieces) + twin + 3,
        scratch=[pltpu.VMEM((twin, tokens // twin, entries), F32), pltpu.VMEM((tokens // twin, 128), F32)],
        us=2.0,
    )(*pieces, unembed, *others, target_column, weights, in_part)
    partial = lax.all_to_all(partial, AXES, 0, 0, tiled=True)
    partial = partial.reshape(n_dp // twin, twin, n_vocab, 4 * per_device, projected)
    merged, logprob = call(
        functools.partial(merge_kernel, features),
        (sds((devices, 2 * per_device, projected), BF16), sds((1, rows), F32)),
        3,
    )(partial, hidden_proj, root_mean)
    merged = lax.all_to_all(merged, AXES, 0, 0, tiled=True)
    padded = -(-seqs // 8) * 8
    scores = call(
        scores_kernel,
        sds((seqs, store.shape[0]), F32),
        3,
        scratch=(
            pltpu.VMEM((tokens, projected), F32),
            pltpu.VMEM((tokens, projected), F32),
            pltpu.VMEM((projected * padded, tokens), F32),
            pltpu.VMEM((padded, store.shape[1]), F32),
        ),
    )(merged, segment_ids.reshape(1, tokens), store)
    return scores, logprob.reshape(rows)


def solution(mesh):
    size = dict(mesh.shape)
    in_specs = (
        P("dp", "vocab"),
        P("dp", "vocab"),
        P(),
        P(AXES, None),
        P(),
        P(),
        P(),
        P(),
        P(AXES, None),
    )
    out_specs = (P(None, AXES), P("dp"))
    return jax.shard_map(
        functools.partial(body, size), mesh=mesh, in_specs=in_specs, out_specs=out_specs, check_vma=False
    )
```

```python
import functools

import jax
import jax.numpy as jnp
from jax import lax
from jax.experimental import pallas as pl
from jax.experimental.pallas import tpu as pltpu
from jax.sharding import PartitionSpec as P


EPSILON = 1e-06
AXES = ("dp", "vocab")
F32 = jnp.float32
BF16 = jnp.bfloat16


VMEM = pl.BlockSpec(memory_space=pltpu.VMEM)
HBM = pl.BlockSpec(memory_space=pltpu.HBM)


def split(x):
    high = x.astype(BF16)
    return high, (x - high.astype(F32)).astype(BF16)


def dot(a, b, dims=((1,), (0,))):
    return lax.dot_general(a, b, (dims, ((), ())), preferred_element_type=F32)


def call(kernel, out_shape, n_in, hbm_at=(), scratch=(), us=1.0):
    specs = [HBM if i in hbm_at else VMEM for i in range(n_in)]
    outs = jax.tree.map(lambda _: VMEM, out_shape)
    run = pl.pallas_call(
        kernel,
        out_shape=out_shape,
        in_specs=specs,
        out_specs=outs,
        scratch_shapes=list(scratch),
        cost_estimate=pl.CostEstimate(flops=0, transcendentals=0, bytes_accessed=int(us * 3_000_000)),
        compiler_params=pltpu.CompilerParams(vmem_limit_bytes=32 * 1024 * 1024),
    )

    def placed(*args):
        return run(
            *[pltpu.with_memory_space_constraint(x, pltpu.HBM) if i in hbm_at else x for i, x in enumerate(args)]
        )

    return placed


def stage_kernel(*refs):
    n = len(refs) // 2
    sources, targets, sems = refs[:n], refs[n : 2 * n], refs[2 * n]
    copies = []
    for i, (source, target) in enumerate(zip(sources, targets, strict=True)):
        if source.shape != target.shape:
            width = target.shape[0]
            source = source.at[pl.ds(pl.multiple_of(lax.axis_index("vocab") * width, 16), width), :]
        copies.append(pltpu.make_async_copy(source, target, sems.at[i]))
    for copy in copies:
        copy.start()
    for copy in copies:
        copy.wait()


def norm_kernel(offsets, *refs):
    pieces, gain, normed, root_mean = refs[:-3], refs[-3], refs[-2], refs[-1]
    squares, features = 0.0, 0
    for piece in pieces:
        wide = piece[...].astype(F32)
        squares = squares + jnp.sum(wide * wide, axis=1, keepdims=True)
        features += wide.shape[1]
    root = jnp.sqrt(squares / features + EPSILON)
    inverse = 1.0 / root
    for piece, offset in zip(pieces, offsets, strict=True):
        width = piece.shape[1]
        here = pl.ds(pl.multiple_of(offset(), 128), width)
        normed[:, here] = (piece[...].astype(F32) * gain[:, here] * inverse).astype(BF16)
    wide_root = jnp.broadcast_to(root, (root.shape[0], 128))
    chunks, rows, _ = root_mean.shape
    for c in range(chunks):
        root_mean[c] = wide_root[c * rows : (c + 1) * rows]


def side_kernel(offsets, others, *refs):
    n = len(offsets)
    pieces, other_unembeds, refs = refs[:n], refs[n : n + others], refs[n + others :]
    proj_out, unembed, proj_slice, inputs, targets, gain, weights, in_part, hidden_proj, target_column = refs
    total = 0.0
    for piece, offset in zip(pieces, offsets, strict=True):
        width = piece.shape[1]
        total = total + dot(piece[...], proj_out[pl.ds(pl.multiple_of(offset(), 16), width), :])
    for u, rows_of in enumerate((unembed, *other_unembeds)):
        scaled_high, scaled_low = split(rows_of[...].astype(F32) * gain[...])
        weights[u] = dot(scaled_high, proj_out[...]) + dot(scaled_low, proj_out[...])
    tokens = targets.shape[1]
    target_column[...] = jnp.broadcast_to(targets[...].astype(F32), (128, tokens)).T
    part = dot(inputs[...], proj_slice[...])
    chunks, rows, _ = in_part.shape
    for c in range(chunks):
        in_part[c] = part[c * rows : (c + 1) * rows]
        hidden_proj[c] = total[c * rows : (c + 1) * rows]


def logits_kernel(order, twin, *refs):
    n = len(order)
    pieces, unembeds = refs[:n], refs[n : n + twin]
    target_column, weights, in_part, out, placed, placed_target = refs[n + twin :]
    rows = pieces[0].shape[0]
    normed = jnp.concatenate([piece[...] for piece in pieces], axis=0)
    entries = unembeds[0].shape[0]
    mine, own = lax.axis_index("dp"), lax.axis_size("vocab")
    starts = [(pl.multiple_of(local(), 16), pl.multiple_of(whole(), 16)) for local, whole in order]
    for local, whole in starts:
        placed_target[pl.ds(local, rows), :] = target_column[pl.ds(whole, rows), :]
    logits, onehot = [], []
    for u, unembed in enumerate(unembeds):
        relative = dot(unembed[...], normed, ((1,), (1,))).T
        for k, (local, _) in enumerate(starts):
            placed[u, pl.ds(local, rows), :] = relative[k * rows : (k + 1) * rows]
        logits.append(placed[u])
        place = (mine ^ u) * own + lax.axis_index("vocab")
        column = lax.broadcasted_iota(jnp.int32, relative.shape, 1) + place * entries
        onehot.append(placed_target[:, 0:1] == column.astype(F32))
    tokens = logits[0].shape[0]
    peak = functools.reduce(jnp.maximum, [jnp.max(x, axis=1, keepdims=True) for x in logits])
    total = moment = target_logit = sums = target_row = 0.0
    for u in range(twin):
        shifted = logits[u] - peak
        other = jnp.where(onehot[u], 0.0, jnp.exp(shifted))
        total = total + jnp.sum(other, axis=1, keepdims=True)
        moment = moment + jnp.sum(other * shifted, axis=1, keepdims=True)
        target_logit = target_logit + jnp.sum(jnp.where(onehot[u], logits[u], 0.0), axis=1, keepdims=True)
        w_high, w_low = split(weights[u])
        p_high, p_low = split(other)
        sums = sums + (dot(p_high, w_high) + (dot(p_high, w_low) + dot(p_low, w_high)))
        hot = onehot[u].astype(F32).astype(BF16)
        target_row = target_row + dot(hot, w_high)
    lane = lax.broadcasted_iota(jnp.int32, (tokens, 128), 1)
    which = (lane // 2) % 4
    stats = jnp.where(which < 2, jnp.where(which == 0, peak, total), jnp.where(which == 2, moment, target_logit))
    high = stats.astype(BF16).astype(F32)
    middle = (stats - high).astype(BF16).astype(F32)
    low = stats - high - middle
    piece = (lane // 8) % 4
    stats = jnp.where(piece == 0, high, jnp.where(piece == 1, middle, jnp.where(piece == 2, low, 0.0)))
    chunks = out.shape[0]
    rows = tokens * twin // chunks
    block = lax.broadcasted_iota(jnp.int32, (rows, 128), 1) // (128 // own)
    for d in range(chunks // own):
        first = d // twin * own
        row_stats = stats[first * rows : (first + 1) * rows]
        for k in range(1, own):
            row_stats = jnp.where(block == k, stats[(first + k) * rows : (first + k + 1) * rows], row_stats)
        for k in range(own):
            here = slice((first + k) * rows, (first + k + 1) * rows)
            terms = jnp.where(mine == d, in_part[k], 0.0)
            packed = jnp.concatenate([sums[here], target_row[here], terms, row_stats], axis=0)
            out[d * own + k] = packed.astype(BF16)


def merge_kernel(features, parts, hidden_projs, root_means, out, logprob):
    index, own = lax.axis_index("vocab"), lax.axis_size("vocab")
    hidden_proj = hidden_projs[index]
    root_mean = root_means[index]
    rows = hidden_proj.shape[0]
    chunks = parts.shape[0] * own
    received = parts[:, lax.axis_index("dp") % parts.shape[1]]
    received = received.reshape(chunks, *received.shape[2:]).astype(F32)
    stats = received[:, 3 * rows : 4 * rows].reshape(chunks * rows, 128)
    stats = stats + pltpu.roll(stats, 128 - 8, 1) + pltpu.roll(stats, 128 - 16, 1)
    shape = (chunks, rows, 128)
    peak, total = stats.reshape(shape), pltpu.roll(stats, 128 - 2, 1).reshape(shape)
    moment = pltpu.roll(stats, 128 - 4, 1).reshape(shape)
    target_logit = jnp.sum(pltpu.roll(stats, 128 - 6, 1).reshape(shape), axis=0)
    row_peak = jnp.max(peak, axis=0)
    scale = jnp.exp(peak - row_peak[None])
    row_total = jnp.sum(scale * total, axis=0) + jnp.exp(target_logit - row_peak)
    weight = scale / row_total[None]
    rest = jnp.sum(weight * total, axis=0)
    slope = jnp.sum(weight * (total * (target_logit[None] - peak) - moment), axis=0)
    log_of = target_logit - row_peak - jnp.log(row_total)
    group = 128 // own
    lane = lax.broadcasted_iota(jnp.int32, (rows, 128), 1)
    row = lax.broadcasted_iota(jnp.int32, (rows, 128), 0)
    spread = jnp.zeros((rows, 128), F32)
    for k in range(own):
        spread = jnp.where(lane == k * rows + row, log_of[:, k * group : k * group + 1], spread)
    logprob[...] = jnp.sum(spread, axis=0, keepdims=True)[:, 0 : logprob.shape[1]]

    def pick(x):
        at = lax.broadcasted_iota(jnp.int32, x.shape, x.ndim - 1) == index * group
        return jnp.sum(jnp.where(at, x, 0.0), axis=-1, keepdims=True)

    weight, rest, slope = pick(weight), pick(rest), pick(slope)
    target_row = jnp.sum(received[:, rows : 2 * rows], axis=0)
    grad_proj = rest * target_row - jnp.sum(weight * received[:, 0:rows], axis=0)
    grad_dot = root_mean * slope
    out_grad = grad_proj / root_mean - hidden_proj * (
        grad_dot / (features * (root_mean * root_mean * root_mean))
    )
    in_proj = jnp.sum(received[:, 2 * rows : 3 * rows], axis=0)
    both = jnp.concatenate([out_grad, in_proj], axis=0).astype(BF16)
    out[...] = jnp.broadcast_to(both[None], out.shape)


def scores_kernel(parts, segments, store, logprob_in, scores, logprob, out_grad, in_proj, spread, flat):
    logprob[...] = logprob_in[...]
    chunks, rows = parts.shape[0], parts.shape[1] // 2
    for c in range(chunks):
        both = parts[c].astype(F32)
        here = slice(c * rows, (c + 1) * rows)
        out_grad[here, :] = both[0:rows]
        in_proj[here, :] = both[rows : 2 * rows]
    turned = out_grad[...].T
    tokens = turned.shape[1]
    seqs = flat.shape[0]
    member = (segments[...] == lax.broadcasted_iota(jnp.int32, (seqs, tokens), 0)).astype(F32)
    for p in range(turned.shape[0]):
        spread[p * seqs : (p + 1) * seqs, :] = turned[p : p + 1, :] * member
    grads = dot(spread[...].astype(BF16), in_proj[...].astype(BF16))
    width = grads.shape[1]
    for p in range(turned.shape[0]):
        flat[:, p * width : (p + 1) * width] = grads[p * seqs : (p + 1) * seqs, :]
    result = dot(flat[...].astype(BF16), store[...], ((1,), (1,)))
    scores[...] = result[0 : scores.shape[0], :]


def swap(x, size, mask):
    vocab = size["vocab"]
    count = size["dp"] * vocab
    return lax.ppermute(x, AXES, [(i, i ^ mask) for i in range(count)])


def body(size, *args):
    return steps(size, *args)


def steps(size, hidden, inputs, gain, unembed, proj_out, proj_in, targets, segment_ids, store):
    n_dp, n_vocab = size["dp"], size["vocab"]
    devices = n_dp * n_vocab
    tokens, features = targets.shape[0], gain.shape[0]
    per_device = tokens // devices
    rows, width = hidden.shape
    seqs = tokens // 32
    entries = unembed.shape[0]
    projected = proj_out.shape[1]
    gain_row = gain.reshape(1, features)

    sds = jax.ShapeDtypeStruct
    fast = n_dp == 8 and n_vocab == 4 and width % 128 == 0
    twin = 2 if fast else 1
    row_shape = sds((n_vocab, per_device, projected), F32)

    def norm(row_pieces, offsets):
        return call(
            functools.partial(norm_kernel, offsets), (sds((rows, features), BF16), row_shape), len(row_pieces) + 1
        )(*row_pieces, gain_row)

    sources = (hidden, gain_row, proj_out, unembed, proj_in, inputs, targets.reshape(1, tokens))
    shapes = [sds(x.shape, x.dtype) for x in sources]
    shapes[4] = sds((inputs.shape[1], projected), BF16)
    hidden_here, gain_row, proj_out, unembed_here, proj_slice, inputs, target_row = call(
        stage_kernel,
        tuple(shapes),
        len(sources),
        hbm_at=range(len(sources)),
        scratch=[pltpu.SemaphoreType.DMA((len(sources),))],
    )(*sources)

    def side_work(row_pieces, offsets, others):
        return call(
            functools.partial(side_kernel, offsets, len(others)),
            (sds((twin, entries, projected), F32), row_shape, row_shape, sds((tokens, 128), F32)),
            len(row_pieces) + len(others) + 6,
            us=4.0,
        )(*row_pieces, *others, proj_out, unembed_here, proj_slice, inputs, target_row, gain_row)

    if fast:
        row_pieces = [swap(hidden, size, k) for k in (2, 3, 1)]
        others = [swap(unembed, size, n_vocab)]
        row_pieces = [hidden_here] + row_pieces
        offsets = [lambda k=k: (lax.axis_index("vocab") ^ k) * width for k in (0, 2, 3, 1)]
        normed, root_mean = norm(row_pieces, offsets)
        *row_pieces, _ = lax.optimization_barrier((*row_pieces, normed))
        side = side_work(row_pieces, offsets, others)
        masks = (0, 6, 4, 2)
        pieces = [normed] + [swap(normed, size, r * n_vocab) for r in masks[1:]]
        order = [
            (
                lambda r=r: (lax.axis_index("dp") ^ r) // 2 * rows,
                lambda r=r: (lax.axis_index("dp") ^ r) * rows,
            )
            for r in masks
        ]
    else:
        row_pieces = [lax.all_gather(hidden, "vocab", axis=1, tiled=True)]
        offsets, others = [lambda: 0], []
        normed, root_mean = norm(row_pieces, offsets)
        side = side_work(row_pieces, offsets, others)
        pieces = [lax.all_gather(normed, "dp", axis=0, tiled=True)]
        order = [(lambda: 0, lambda: 0)]
    weights, in_part, hidden_proj, target_column = side
    partial = call(
        functools.partial(logits_kernel, order, twin),
        sds((devices, 4 * per_device, projected), BF16),
        len(pieces) + twin + 3,
        scratch=[pltpu.VMEM((twin, tokens // twin, entries), F32), pltpu.VMEM((tokens // twin, 128), F32)],
        us=2.0,
    )(*pieces, unembed_here, *others, target_column, weights, in_part)
    partial = lax.all_to_all(partial, AXES, 0, 0, tiled=True)
    partial = partial.reshape(n_dp // twin, twin, n_vocab, 4 * per_device, projected)
    merged, logprob = call(
        functools.partial(merge_kernel, features),
        (sds((devices, 2 * per_device, projected), BF16), sds((1, rows), F32)),
        3,
    )(partial, hidden_proj, root_mean)
    merged = lax.all_to_all(merged, AXES, 0, 0, tiled=True)
    padded = -(-seqs // 8) * 8
    scores, logprob = call(
        scores_kernel,
        (sds((seqs, store.shape[0]), F32), sds((1, rows), F32)),
        4,
        scratch=(
            pltpu.VMEM((tokens, projected), F32),
            pltpu.VMEM((tokens, projected), F32),
            pltpu.VMEM((projected * padded, tokens), F32),
            pltpu.VMEM((padded, store.shape[1]), F32),
        ),
    )(merged, segment_ids.reshape(1, tokens), store, logprob)
    return scores, logprob.reshape(rows)


def solution(mesh):
    size = dict(mesh.shape)
    in_specs = (
        P("dp", "vocab"),
        P("dp", "vocab"),
        P(),
        P(AXES, None),
        P(),
        P(),
        P(),
        P(),
        P(AXES, None),
    )
    out_specs = (P(None, AXES), P("dp"))
    return jax.shard_map(
        functools.partial(body, size), mesh=mesh, in_specs=in_specs, out_specs=out_specs, check_vma=False
    )
```

```python
import functools

import jax
import jax.numpy as jnp
from jax import lax
from jax.experimental import pallas as pl
from jax.experimental.pallas import tpu as pltpu
from jax.sharding import PartitionSpec as P


EPSILON = 1e-06
AXES = ("dp", "vocab")
F32 = jnp.float32
BF16 = jnp.bfloat16


VMEM = pl.BlockSpec(memory_space=pltpu.VMEM)
HBM = pl.BlockSpec(memory_space=pltpu.HBM)


def split(x):
    high = x.astype(BF16)
    return high, (x - high.astype(F32)).astype(BF16)


def dot(a, b, dims=((1,), (0,))):
    return lax.dot_general(a, b, (dims, ((), ())), preferred_element_type=F32)


def call(kernel, out_shape, n_in, hbm_at=(), scratch=(), us=1.0):
    specs = [HBM if i in hbm_at else VMEM for i in range(n_in)]
    outs = jax.tree.map(lambda _: VMEM, out_shape)
    run = pl.pallas_call(
        kernel,
        out_shape=out_shape,
        in_specs=specs,
        out_specs=outs,
        scratch_shapes=list(scratch),
        cost_estimate=pl.CostEstimate(flops=0, transcendentals=0, bytes_accessed=int(us * 3_000_000)),
        compiler_params=pltpu.CompilerParams(vmem_limit_bytes=32 * 1024 * 1024),
    )

    def placed(*args):
        return run(
            *[pltpu.with_memory_space_constraint(x, pltpu.HBM) if i in hbm_at else x for i, x in enumerate(args)]
        )

    return placed


def stage_kernel(*refs):
    n = len(refs) // 2
    sources, targets, sems = refs[:n], refs[n : 2 * n], refs[2 * n]
    copies = [
        pltpu.make_async_copy(source, target, sems.at[i])
        for i, (source, target) in enumerate(zip(sources, targets, strict=True))
    ]
    for copy in copies:
        copy.start()
    for copy in copies:
        copy.wait()


def norm_kernel(offsets, *refs):
    n = len(offsets)
    pieces, gain, root_mean, own, rest = refs[:n], refs[n], refs[n + 1], refs[n + 2], refs[n + 3 :]
    squares, features = 0.0, 0
    for piece in pieces:
        wide = piece[...].astype(F32)
        squares = squares + jnp.sum(wide * wide, axis=1, keepdims=True)
        features += wide.shape[1]
    root = jnp.sqrt(squares / features + EPSILON)
    inverse = 1.0 / root
    for k, (piece, offset) in enumerate(zip(pieces, offsets, strict=True)):
        width = piece.shape[1]
        here = pl.ds(pl.multiple_of(offset(), 128), width)
        value = (piece[...].astype(F32) * gain[:, here] * inverse).astype(BF16)
        if k:
            for target in rest:
                target[:, (k - 1) * width : k * width] = value
        else:
            own[...] = value
            if rest:
                rest[1][:, -width:] = value
    if rest:
        lane = lax.broadcasted_iota(jnp.int32, (root.shape[0], 128), 1)
        high = inverse.astype(BF16).astype(F32)
        middle = (inverse - high).astype(BF16).astype(F32)
        low = inverse - high - middle
        rest[0][:, -128:] = jnp.where(lane < 32, high, jnp.where(lane < 64, middle, low)).astype(BF16)
    wide_root = jnp.broadcast_to(root, (root.shape[0], 128))
    chunks, rows, _ = root_mean.shape
    for c in range(chunks):
        root_mean[c] = wide_root[c * rows : (c + 1) * rows]


def side_kernel(offsets, others, *refs):
    n = len(offsets)
    pieces, other_unembeds, refs = refs[:n], refs[n : n + others], refs[n + others :]
    sources, gain = refs[:5], refs[5]
    weights, in_part, hidden_proj, target_column = refs[6:10]
    buffers, sems = refs[10:15], refs[15]
    copies = []
    for i, (source, buffer) in enumerate(zip(sources, buffers, strict=True)):
        if source.shape != buffer.shape:
            width = buffer.shape[0]
            source = source.at[pl.ds(pl.multiple_of(lax.axis_index("vocab") * width, 16), width), :]
        copies.append(pltpu.make_async_copy(source, buffer, sems.at[i]))
        copies[-1].start()
    proj_out, unembed, proj_slice, inputs, targets = buffers
    copies[0].wait()
    total = 0.0
    for piece, offset in zip(pieces, offsets, strict=True):
        width = piece.shape[1]
        total = total + dot(piece[...], proj_out[pl.ds(pl.multiple_of(offset(), 16), width), :])
    for u, rows_of in reversed(list(enumerate((unembed, *other_unembeds)))):
        if u == 0:
            copies[1].wait()
        weights[u] = dot((rows_of[...].astype(F32) * gain[...]).astype(BF16), proj_out[...])
    for copy in copies[2:]:
        copy.wait()
    tokens = targets.shape[1]
    target_column[...] = jnp.broadcast_to(targets[...].astype(F32), (128, tokens)).T
    part = dot(inputs[...], proj_slice[...])
    chunks, rows, _ = in_part.shape
    for c in range(chunks):
        in_part[c] = part[c * rows : (c + 1) * rows]
        hidden_proj[c] = total[c * rows : (c + 1) * rows]


def logits_kernel(order, twin, offsets, *refs):
    n = len(order)
    own, refs = refs[0], refs[1:]
    rows, width = own.shape
    blocks = [[own[...]]]
    if n > 1:
        count = n - 2
        early, parts, gain, refs = refs[:count], refs[count : count + n], refs[count + n], refs[count + n + 1 :]
        own_gain = gain[:, pl.ds(pl.multiple_of(offsets[0](), 128), width)]
        for raw, part in zip(early, parts[1:-1], strict=True):
            tail = part[:, -128:].astype(F32)
            inverse = tail[:, 0:1] + tail[:, 32:33] + tail[:, 64:65]
            blocks[0].append((raw[...].astype(F32) * own_gain * inverse).astype(BF16))
        blocks[0].append(parts[-1][:, -width:])
        for k in range(1, len(offsets)):
            blocks.append([part[:, (k - 1) * width : k * width] for part in parts])
    unembeds = refs[:twin]
    target_column, weights, in_part, out, placed, placed_target = refs[twin:]
    blocks = [jnp.concatenate(block, axis=0) for block in blocks]
    slices = [pl.ds(pl.multiple_of(offset(), 128), width) for offset in offsets]
    entries = unembeds[0].shape[0]
    mine, own = lax.axis_index("dp"), lax.axis_size("vocab")
    starts = [(pl.multiple_of(local(), 16), pl.multiple_of(whole(), 16)) for local, whole in order]
    for local, whole in starts:
        placed_target[pl.ds(local, rows), :] = target_column[pl.ds(whole, rows), :]
    logits, onehot = [], []
    for u, unembed in enumerate(unembeds):
        relative = sum(dot(unembed[:, at], block, ((1,), (1,))) for at, block in zip(slices, blocks, strict=True)).T
        for k, (local, _) in enumerate(starts):
            placed[u, pl.ds(local, rows), :] = relative[k * rows : (k + 1) * rows]
        logits.append(placed[u])
        place = (mine ^ u) * own + lax.axis_index("vocab")
        column = lax.broadcasted_iota(jnp.int32, relative.shape, 1) + place * entries
        onehot.append(placed_target[:, 0:1] == column.astype(F32))
    tokens = logits[0].shape[0]
    peak = functools.reduce(jnp.maximum, [jnp.max(x, axis=1, keepdims=True) for x in logits])
    total = moment = target_logit = sums = target_row = 0.0
    for u in range(twin):
        shifted = logits[u] - peak
        other = jnp.where(onehot[u], 0.0, jnp.exp(shifted))
        total = total + jnp.sum(other, axis=1, keepdims=True)
        moment = moment + jnp.sum(other * shifted, axis=1, keepdims=True)
        target_logit = target_logit + jnp.sum(jnp.where(onehot[u], logits[u], 0.0), axis=1, keepdims=True)
        w_high, w_low = split(weights[u])
        p_high, p_low = split(other)
        sums = sums + (dot(p_high, w_high) + (dot(p_high, w_low) + dot(p_low, w_high)))
        hot = onehot[u].astype(F32).astype(BF16)
        target_row = target_row + dot(hot, w_high)
    lane = lax.broadcasted_iota(jnp.int32, (tokens, 128), 1)
    which = (lane // 2) % 4
    stats = jnp.where(which < 2, jnp.where(which == 0, peak, total), jnp.where(which == 2, moment, target_logit))
    high = stats.astype(BF16).astype(F32)
    middle = (stats - high).astype(BF16).astype(F32)
    low = stats - high - middle
    piece = (lane // 8) % 4
    stats = jnp.where(piece == 0, high, jnp.where(piece == 1, middle, jnp.where(piece == 2, low, 0.0)))
    chunks = out.shape[0]
    rows = tokens * twin // chunks
    block = lax.broadcasted_iota(jnp.int32, (rows, 128), 1) // (128 // own)
    for d in range(chunks // own):
        first = d // twin * own
        row_stats = stats[first * rows : (first + 1) * rows]
        for k in range(1, own):
            row_stats = jnp.where(block == k, stats[(first + k) * rows : (first + k + 1) * rows], row_stats)
        for k in range(own):
            here = slice((first + k) * rows, (first + k + 1) * rows)
            terms = jnp.where(mine == d, in_part[k], 0.0)
            packed = jnp.concatenate([sums[here], target_row[here], terms, row_stats], axis=0)
            out[d * own + k] = packed.astype(BF16)


def merge_kernel(features, parts, hidden_projs, root_means, out, logprob):
    index, own = lax.axis_index("vocab"), lax.axis_size("vocab")
    hidden_proj = hidden_projs[index]
    root_mean = root_means[index]
    rows = hidden_proj.shape[0]
    chunks = parts.shape[0] * own
    received = parts[:, lax.axis_index("dp") % parts.shape[1]]
    received = received.reshape(chunks, *received.shape[2:]).astype(F32)
    stats = received[:, 3 * rows : 4 * rows].reshape(chunks * rows, 128)
    stats = stats + pltpu.roll(stats, 128 - 8, 1) + pltpu.roll(stats, 128 - 16, 1)
    shape = (chunks, rows, 128)
    peak, total = stats.reshape(shape), pltpu.roll(stats, 128 - 2, 1).reshape(shape)
    moment = pltpu.roll(stats, 128 - 4, 1).reshape(shape)
    target_logit = jnp.sum(pltpu.roll(stats, 128 - 6, 1).reshape(shape), axis=0)
    row_peak = jnp.max(peak, axis=0)
    scale = jnp.exp(peak - row_peak[None])
    row_total = jnp.sum(scale * total, axis=0) + jnp.exp(target_logit - row_peak)
    weight = scale / row_total[None]
    rest = jnp.sum(weight * total, axis=0)
    slope = jnp.sum(weight * (total * (target_logit[None] - peak) - moment), axis=0)
    log_of = target_logit - row_peak - jnp.log(row_total)
    group = 128 // own
    lane = lax.broadcasted_iota(jnp.int32, (rows, 128), 1)
    row = lax.broadcasted_iota(jnp.int32, (rows, 128), 0)
    spread = jnp.zeros((rows, 128), F32)
    for k in range(own):
        spread = jnp.where(lane == k * rows + row, log_of[:, k * group : k * group + 1], spread)
    logprob[...] = jnp.sum(spread, axis=0, keepdims=True)[:, 0 : logprob.shape[1]]

    def pick(x):
        at = lax.broadcasted_iota(jnp.int32, x.shape, x.ndim - 1) == index * group
        return jnp.sum(jnp.where(at, x, 0.0), axis=-1, keepdims=True)

    weight, rest, slope = pick(weight), pick(rest), pick(slope)
    target_row = jnp.sum(received[:, rows : 2 * rows], axis=0)
    grad_proj = rest * target_row - jnp.sum(weight * received[:, 0:rows], axis=0)
    grad_dot = root_mean * slope
    out_grad = grad_proj / root_mean - hidden_proj * (
        grad_dot / (features * (root_mean * root_mean * root_mean))
    )
    in_proj = jnp.sum(received[:, 2 * rows : 3 * rows], axis=0)
    both = jnp.concatenate([out_grad, in_proj], axis=0).astype(BF16)
    out[...] = jnp.broadcast_to(both[None], out.shape)


def scores_kernel(parts, segments, store, logprob_in, scores, logprob, out_grad, in_proj, spread, flat):
    logprob[...] = logprob_in[...]
    chunks, rows = parts.shape[0], parts.shape[1] // 2
    for c in range(chunks):
        both = parts[c].astype(F32)
        here = slice(c * rows, (c + 1) * rows)
        out_grad[here, :] = both[0:rows]
        in_proj[here, :] = both[rows : 2 * rows]
    turned = out_grad[...].T
    tokens = turned.shape[1]
    seqs = flat.shape[0]
    member = (segments[...] == lax.broadcasted_iota(jnp.int32, (seqs, tokens), 0)).astype(F32)
    for p in range(turned.shape[0]):
        spread[p * seqs : (p + 1) * seqs, :] = turned[p : p + 1, :] * member
    grads = dot(spread[...].astype(BF16), in_proj[...].astype(BF16))
    width = grads.shape[1]
    for p in range(turned.shape[0]):
        flat[:, p * width : (p + 1) * width] = grads[p * seqs : (p + 1) * seqs, :]
    result = dot(flat[...].astype(BF16), store[...], ((1,), (1,)))
    scores[...] = result[0 : scores.shape[0], :]


def swap(x, size, mask):
    return lax.ppermute(x, AXES, [(i, i ^ mask) for i in range(size["dp"] * size["vocab"])])


def body(size, *args):
    return steps(size, *args)


def steps(size, hidden, inputs, gain, unembed, proj_out, proj_in, targets, segment_ids, store):
    n_dp, n_vocab = size["dp"], size["vocab"]
    devices = n_dp * n_vocab
    tokens, features = targets.shape[0], gain.shape[0]
    per_device = tokens // devices
    rows, width = hidden.shape
    seqs = tokens // 32
    entries = unembed.shape[0]
    projected = proj_out.shape[1]
    gain_row = gain.reshape(1, features)

    sds = jax.ShapeDtypeStruct
    fast = n_dp == 8 and n_vocab == 4 and width % 128 == 0
    twin = 2 if fast else 1
    row_shape = sds((n_vocab, per_device, projected), F32)

    def norm(row_pieces, offsets, rest=()):
        return call(
            functools.partial(norm_kernel, offsets),
            (row_shape, sds((rows, row_pieces[0].shape[1]), BF16), *rest),
            len(row_pieces) + 1,
        )(*row_pieces, gain_row)

    hidden_here, gain_row = call(
        stage_kernel,
        (sds(hidden.shape, BF16), sds(gain_row.shape, F32)),
        2,
        hbm_at=(0, 1),
        scratch=[pltpu.SemaphoreType.DMA((2,))],
    )(hidden, gain_row)

    def side_work(row_pieces, offsets, others):
        n = len(row_pieces) + len(others)
        sources = (proj_out, unembed, proj_in, inputs, targets.reshape(1, tokens))
        shapes = [pltpu.VMEM(x.shape, x.dtype) for x in sources]
        shapes[2] = pltpu.VMEM((inputs.shape[1], projected), BF16)
        return call(
            functools.partial(side_kernel, offsets, len(others)),
            (sds((twin, entries, projected), F32), row_shape, row_shape, sds((tokens, 128), F32)),
            n + 6,
            hbm_at=range(n, n + 5),
            scratch=shapes + [pltpu.SemaphoreType.DMA((5,))],
            us=4.0,
        )(*row_pieces, *others, *sources, gain_row)

    if fast:
        row_pieces = [swap(hidden, size, k) for k in (2, 3, 1)]
        masks = (0, 6, 4, 2)
        early = [swap(hidden, size, r * n_vocab) for r in masks[1:-1]]
        others = [swap(unembed, size, n_vocab)]
        row_pieces = [hidden_here] + row_pieces
        offsets = [lambda k=k: (lax.axis_index("vocab") ^ k) * width for k in (0, 2, 3, 1)]
        shapes = sds((rows, features - width + 128), BF16), sds((rows, features), BF16)
        root_mean, own, rest, whole = norm(row_pieces, offsets, shapes)
        *row_pieces, _ = lax.optimization_barrier((*row_pieces, own))
        side = side_work(row_pieces, offsets, others)
        late = [swap(rest, size, r * n_vocab) for r in masks[1:-1]]
        late.append(swap(whole, size, masks[-1] * n_vocab))
        pieces = [own, *early, rest, *late, gain_row]
        order = [
            (
                lambda r=r: (lax.axis_index("dp") ^ r) // 2 * rows,
                lambda r=r: (lax.axis_index("dp") ^ r) * rows,
            )
            for r in masks
        ]
    else:
        row_pieces = [lax.all_gather(hidden, "vocab", axis=1, tiled=True)]
        offsets, others = [lambda: 0], []
        root_mean, own = norm(row_pieces, offsets)
        side = side_work(row_pieces, offsets, others)
        pieces = [lax.all_gather(own, "dp", axis=0, tiled=True)]
        order = [(lambda: 0, lambda: 0)]
    weights, in_part, hidden_proj, target_column = side
    partial = call(
        functools.partial(logits_kernel, order, twin, offsets),
        sds((devices, 4 * per_device, projected), BF16),
        len(pieces) + twin + 3,
        scratch=[pltpu.VMEM((twin, tokens // twin, entries), F32), pltpu.VMEM((tokens // twin, 128), F32)],
        us=2.0,
    )(*pieces, unembed, *others, target_column, weights, in_part)
    partial = lax.all_to_all(partial, AXES, 0, 0, tiled=True)
    partial = partial.reshape(n_dp // twin, twin, n_vocab, 4 * per_device, projected)
    merged, logprob = call(
        functools.partial(merge_kernel, features),
        (sds((devices, 2 * per_device, projected), BF16), sds((1, rows), F32)),
        3,
    )(partial, hidden_proj, root_mean)
    merged = lax.all_to_all(merged, AXES, 0, 0, tiled=True)
    padded = -(-seqs // 8) * 8
    scores, logprob = call(
        scores_kernel,
        (sds((seqs, store.shape[0]), F32), sds((1, rows), F32)),
        4,
        scratch=(
            pltpu.VMEM((tokens, projected), F32),
            pltpu.VMEM((tokens, projected), F32),
            pltpu.VMEM((projected * padded, tokens), F32),
            pltpu.VMEM((padded, store.shape[1]), F32),
        ),
    )(merged, segment_ids.reshape(1, tokens), store, logprob)
    return scores, logprob.reshape(rows)


def solution(mesh):
    size = dict(mesh.shape)
    in_specs = (
        P("dp", "vocab"),
        P("dp", "vocab"),
        P(),
        P(AXES, None),
        P(),
        P(),
        P(),
        P(),
        P(AXES, None),
    )
    out_specs = (P(None, AXES), P("dp"))
    return jax.shard_map(
        functools.partial(body, size), mesh=mesh, in_specs=in_specs, out_specs=out_specs, check_vma=False
    )
```

```python
import functools

import jax
import jax.numpy as jnp
from jax import lax
from jax.experimental import pallas as pl
from jax.experimental.pallas import tpu as pltpu
from jax.sharding import PartitionSpec as P


EPSILON = 1e-06
AXES = ("dp", "vocab")
F32 = jnp.float32
BF16 = jnp.bfloat16


VMEM = pl.BlockSpec(memory_space=pltpu.VMEM)
HBM = pl.BlockSpec(memory_space=pltpu.HBM)


def split(x):
    high = x.astype(BF16)
    return high, (x - high.astype(F32)).astype(BF16)


def dot(a, b, dims=((1,), (0,))):
    return lax.dot_general(a, b, (dims, ((), ())), preferred_element_type=F32)


def call(kernel, out_shape, n_in, hbm_at=(), scratch=(), us=1.0):
    specs = [HBM if i in hbm_at else VMEM for i in range(n_in)]
    outs = jax.tree.map(lambda _: VMEM, out_shape)
    run = pl.pallas_call(
        kernel,
        out_shape=out_shape,
        in_specs=specs,
        out_specs=outs,
        scratch_shapes=list(scratch),
        cost_estimate=pl.CostEstimate(flops=0, transcendentals=0, bytes_accessed=int(us * 3_000_000)),
        compiler_params=pltpu.CompilerParams(vmem_limit_bytes=32 * 1024 * 1024),
    )

    def placed(*args):
        return run(
            *[pltpu.with_memory_space_constraint(x, pltpu.HBM) if i in hbm_at else x for i, x in enumerate(args)]
        )

    return placed


def stage_kernel(*refs):
    n = len(refs) // 2
    sources, targets, sems = refs[:n], refs[n : 2 * n], refs[2 * n]
    copies = [
        pltpu.make_async_copy(source, target, sems.at[i])
        for i, (source, target) in enumerate(zip(sources, targets, strict=True))
    ]
    for copy in copies:
        copy.start()
    for copy in copies:
        copy.wait()


def norm_kernel(offsets, *refs):
    n = len(offsets)
    pieces, gain, root_mean, own, rest = refs[:n], refs[n], refs[n + 1], refs[n + 2], refs[n + 3 :]
    squares, features = 0.0, 0
    for piece in pieces:
        wide = piece[...].astype(F32)
        squares = squares + jnp.sum(wide * wide, axis=1, keepdims=True)
        features += wide.shape[1]
    root = jnp.sqrt(squares / features + EPSILON)
    inverse = 1.0 / root
    for k, (piece, offset) in enumerate(zip(pieces, offsets, strict=True)):
        width = piece.shape[1]
        here = pl.ds(pl.multiple_of(offset(), 128), width)
        value = (piece[...].astype(F32) * gain[:, here] * inverse).astype(BF16)
        if k:
            for target in rest:
                target[:, (k - 1) * width : k * width] = value
        else:
            own[...] = value
            if rest:
                rest[1][:, -width:] = value
    if rest:
        lane = lax.broadcasted_iota(jnp.int32, (root.shape[0], 128), 1)
        high = inverse.astype(BF16).astype(F32)
        middle = (inverse - high).astype(BF16).astype(F32)
        low = inverse - high - middle
        rest[0][:, -128:] = jnp.where(lane < 32, high, jnp.where(lane < 64, middle, low)).astype(BF16)
    wide_root = jnp.broadcast_to(root, (root.shape[0], 128))
    chunks, rows, _ = root_mean.shape
    for c in range(chunks):
        root_mean[c] = wide_root[c * rows : (c + 1) * rows]


def side_kernel(offsets, others, *refs):
    n = len(offsets)
    pieces, other_unembeds, refs = refs[:n], refs[n : n + others], refs[n + others :]
    sources, gain = refs[:5], refs[5]
    weights, in_part, hidden_proj, target_column = refs[6:10]
    buffers, sems = refs[10:15], refs[15]
    copies = []
    for i, (source, buffer) in enumerate(zip(sources, buffers, strict=True)):
        if source.shape != buffer.shape:
            width = buffer.shape[0]
            source = source.at[pl.ds(pl.multiple_of(lax.axis_index("vocab") * width, 16), width), :]
        copies.append(pltpu.make_async_copy(source, buffer, sems.at[i]))
        copies[-1].start()
    proj_out, unembed, proj_slice, inputs, targets = buffers
    copies[0].wait()
    total = 0.0
    for piece, offset in zip(pieces, offsets, strict=True):
        width = piece.shape[1]
        total = total + dot(piece[...], proj_out[pl.ds(pl.multiple_of(offset(), 16), width), :])
    for u, rows_of in reversed(list(enumerate((unembed, *other_unembeds)))):
        if u == 0:
            copies[1].wait()
        weights[u] = dot((rows_of[...].astype(F32) * gain[...]).astype(BF16), proj_out[...])
    for copy in copies[2:]:
        copy.wait()
    tokens = targets.shape[1]
    target_column[...] = jnp.broadcast_to(targets[...].astype(F32), (128, tokens)).T
    part = dot(inputs[...], proj_slice[...])
    chunks, rows, _ = in_part.shape
    for c in range(chunks):
        in_part[c] = part[c * rows : (c + 1) * rows]
        hidden_proj[c] = total[c * rows : (c + 1) * rows]


def logits_kernel(order, twin, offsets, *refs):
    n = len(order)
    own, refs = refs[0], refs[1:]
    rows, width = own.shape
    blocks = [[own[...]]]
    if n > 1:
        count = n - 2
        early, parts, gain, refs = refs[:count], refs[count : count + n], refs[count + n], refs[count + n + 1 :]
        own_gain = gain[:, pl.ds(pl.multiple_of(offsets[0](), 128), width)]
        for raw, part in zip(early, parts[1:-1], strict=True):
            tail = part[:, -128:].astype(F32)
            inverse = tail[:, 0:1] + tail[:, 32:33] + tail[:, 64:65]
            blocks[0].append((raw[...].astype(F32) * own_gain * inverse).astype(BF16))
        blocks[0].append(parts[-1][:, -width:])
        for k in range(1, len(offsets)):
            blocks.append([part[:, (k - 1) * width : k * width] for part in parts])
    unembeds = refs[:twin]
    target_column, weights, in_part, out = refs[twin:]
    blocks = [jnp.concatenate(block, axis=0) for block in blocks]
    slices = [pl.ds(pl.multiple_of(offset(), 128), width) for offset in offsets]
    entries = unembeds[0].shape[0]
    mine, own_count = lax.axis_index("dp"), lax.axis_size("vocab")
    target = [target_column[pl.ds(pl.multiple_of(whole(), 16), rows), 0:1] for _, whole in order]
    target = jnp.concatenate(target, axis=0)
    logits, onehot = [], []
    for u, unembed in enumerate(unembeds):
        relative = sum(dot(unembed[:, at], block, ((1,), (1,))) for at, block in zip(slices, blocks, strict=True)).T
        logits.append(relative)
        place = (mine ^ u) * own_count + lax.axis_index("vocab")
        column = lax.broadcasted_iota(jnp.int32, relative.shape, 1) + place * entries
        onehot.append(target == column.astype(F32))
    tokens = logits[0].shape[0]
    peak = functools.reduce(jnp.maximum, [jnp.max(x, axis=1, keepdims=True) for x in logits])
    total = moment = target_logit = sums = target_row = 0.0
    for u in range(twin):
        shifted = logits[u] - peak
        other = jnp.where(onehot[u], 0.0, jnp.exp(shifted))
        total = total + jnp.sum(other, axis=1, keepdims=True)
        moment = moment + jnp.sum(other * shifted, axis=1, keepdims=True)
        target_logit = target_logit + jnp.sum(jnp.where(onehot[u], logits[u], 0.0), axis=1, keepdims=True)
        w_high = weights[u].astype(BF16)
        p_high, p_low = split(other)
        hot = onehot[u].astype(F32).astype(BF16)
        stacked = dot(jnp.concatenate([p_high, hot, p_low], axis=0), w_high)
        sums = sums + (stacked[:tokens] + stacked[2 * tokens :])
        target_row = target_row + stacked[tokens : 2 * tokens]
    lane = lax.broadcasted_iota(jnp.int32, (tokens, 128), 1)
    which = (lane // 2) % 4
    stats = jnp.where(which < 2, jnp.where(which == 0, peak, total), jnp.where(which == 2, moment, target_logit))
    high = stats.astype(BF16).astype(F32)
    middle = (stats - high).astype(BF16).astype(F32)
    low = stats - high - middle
    piece = (lane // 8) % 4
    stats = jnp.where(piece == 0, high, jnp.where(piece == 1, middle, jnp.where(piece == 2, low, 0.0)))
    tile = in_part.shape[1]
    block = lax.broadcasted_iota(jnp.int32, (tile, 128), 1) // (128 // own_count)
    for k, (local, _) in enumerate(order):
        for g in range(rows // (own_count * tile)):
            base = k * rows + g * own_count * tile
            row_stats = stats[base : base + tile]
            for c in range(1, own_count):
                row_stats = jnp.where(block == c, stats[base + c * tile : base + (c + 1) * tile], row_stats)
            for e in range(twin):
                row = (local() // (own_count * tile) + g) * twin + e
                for c in range(own_count):
                    here = slice(base + c * tile, base + (c + 1) * tile)
                    terms = jnp.where(mine == row, in_part[c], 0.0)
                    packed = jnp.concatenate([sums[here], target_row[here], terms, row_stats], axis=0)
                    out[row * own_count + c] = packed.astype(BF16)


def merge_kernel(features, parts, hidden_projs, root_means, out, logprob):
    index, own = lax.axis_index("vocab"), lax.axis_size("vocab")
    hidden_proj = hidden_projs[index]
    root_mean = root_means[index]
    rows = hidden_proj.shape[0]
    chunks = parts.shape[0] * own
    received = parts[:, lax.axis_index("dp") % parts.shape[1]]
    received = received.reshape(chunks, *received.shape[2:]).astype(F32)
    stats = received[:, 3 * rows : 4 * rows].reshape(chunks * rows, 128)
    stats = stats + pltpu.roll(stats, 128 - 8, 1) + pltpu.roll(stats, 128 - 16, 1)
    shape = (chunks, rows, 128)
    peak, total = stats.reshape(shape), pltpu.roll(stats, 128 - 2, 1).reshape(shape)
    moment = pltpu.roll(stats, 128 - 4, 1).reshape(shape)
    target_logit = jnp.sum(pltpu.roll(stats, 128 - 6, 1).reshape(shape), axis=0)
    row_peak = jnp.max(peak, axis=0)
    scale = jnp.exp(peak - row_peak[None])
    row_total = jnp.sum(scale * total, axis=0) + jnp.exp(target_logit - row_peak)
    weight = scale / row_total[None]
    rest = jnp.sum(weight * total, axis=0)
    slope = jnp.sum(weight * (total * (target_logit[None] - peak) - moment), axis=0)
    log_of = target_logit - row_peak - jnp.log(row_total)
    group = 128 // own
    lane = lax.broadcasted_iota(jnp.int32, (rows, 128), 1)
    row = lax.broadcasted_iota(jnp.int32, (rows, 128), 0)
    spread = jnp.zeros((rows, 128), F32)
    for k in range(own):
        spread = jnp.where(lane == k * rows + row, log_of[:, k * group : k * group + 1], spread)
    logprob[...] = jnp.sum(spread, axis=0, keepdims=True)[:, 0 : logprob.shape[1]]

    def pick(x):
        at = lax.broadcasted_iota(jnp.int32, x.shape, x.ndim - 1) == index * group
        return jnp.sum(jnp.where(at, x, 0.0), axis=-1, keepdims=True)

    weight, rest, slope = pick(weight), pick(rest), pick(slope)
    target_row = jnp.sum(received[:, rows : 2 * rows], axis=0)
    grad_proj = rest * target_row - jnp.sum(weight * received[:, 0:rows], axis=0)
    grad_dot = root_mean * slope
    out_grad = grad_proj / root_mean - hidden_proj * (
        grad_dot / (features * (root_mean * root_mean * root_mean))
    )
    in_proj = jnp.sum(received[:, 2 * rows : 3 * rows], axis=0)
    both = jnp.concatenate([out_grad, in_proj], axis=0).astype(BF16)
    out[...] = jnp.broadcast_to(both[None], out.shape)


def scores_kernel(parts, segments, store, logprob_in, scores, logprob, out_grad, in_proj, spread, flat):
    logprob[...] = logprob_in[...]
    chunks, rows = parts.shape[0], parts.shape[1] // 2
    for c in range(chunks):
        both = parts[c].astype(F32)
        here = slice(c * rows, (c + 1) * rows)
        out_grad[here, :] = both[0:rows]
        in_proj[here, :] = both[rows : 2 * rows]
    turned = out_grad[...].T
    tokens = turned.shape[1]
    seqs = flat.shape[0]
    member = (segments[...] == lax.broadcasted_iota(jnp.int32, (seqs, tokens), 0)).astype(F32)
    for p in range(turned.shape[0]):
        spread[p * seqs : (p + 1) * seqs, :] = turned[p : p + 1, :] * member
    grads = dot(spread[...].astype(BF16), in_proj[...].astype(BF16))
    width = grads.shape[1]
    for p in range(turned.shape[0]):
        flat[:, p * width : (p + 1) * width] = grads[p * seqs : (p + 1) * seqs, :]
    result = dot(flat[...].astype(BF16), store[...], ((1,), (1,)))
    scores[...] = result[0 : scores.shape[0], :]


def swap(x, size, mask):
    return lax.ppermute(x, AXES, [(i, i ^ mask) for i in range(size["dp"] * size["vocab"])])


def body(size, *args):
    return steps(size, *args)


def steps(size, hidden, inputs, gain, unembed, proj_out, proj_in, targets, segment_ids, store):
    n_dp, n_vocab = size["dp"], size["vocab"]
    devices = n_dp * n_vocab
    tokens, features = targets.shape[0], gain.shape[0]
    per_device = tokens // devices
    rows, width = hidden.shape
    seqs = tokens // 32
    entries = unembed.shape[0]
    projected = proj_out.shape[1]
    gain_row = gain.reshape(1, features)

    sds = jax.ShapeDtypeStruct
    fast = n_dp == 8 and n_vocab == 4 and width % 128 == 0
    twin = 2 if fast else 1
    row_shape = sds((n_vocab, per_device, projected), F32)

    def norm(row_pieces, offsets, rest=()):
        return call(
            functools.partial(norm_kernel, offsets),
            (row_shape, sds((rows, row_pieces[0].shape[1]), BF16), *rest),
            len(row_pieces) + 1,
        )(*row_pieces, gain_row)

    hidden_here, gain_row = call(
        stage_kernel,
        (sds(hidden.shape, BF16), sds(gain_row.shape, F32)),
        2,
        hbm_at=(0, 1),
        scratch=[pltpu.SemaphoreType.DMA((2,))],
    )(hidden, gain_row)

    def side_work(row_pieces, offsets, others):
        n = len(row_pieces) + len(others)
        sources = (proj_out, unembed, proj_in, inputs, targets.reshape(1, tokens))
        shapes = [pltpu.VMEM(x.shape, x.dtype) for x in sources]
        shapes[2] = pltpu.VMEM((inputs.shape[1], projected), BF16)
        return call(
            functools.partial(side_kernel, offsets, len(others)),
            (sds((twin, entries, projected), F32), row_shape, row_shape, sds((tokens, 128), F32)),
            n + 6,
            hbm_at=range(n, n + 5),
            scratch=shapes + [pltpu.SemaphoreType.DMA((5,))],
            us=4.0,
        )(*row_pieces, *others, *sources, gain_row)

    if fast:
        row_pieces = [swap(hidden, size, k) for k in (2, 3, 1)]
        masks = (0, 6, 4, 2)
        early = [swap(hidden, size, r * n_vocab) for r in masks[1:-1]]
        others = [swap(unembed, size, n_vocab)]
        row_pieces = [hidden_here] + row_pieces
        offsets = [lambda k=k: (lax.axis_index("vocab") ^ k) * width for k in (0, 2, 3, 1)]
        shapes = sds((rows, features - width + 128), BF16), sds((rows, features), BF16)
        root_mean, own, rest, whole = norm(row_pieces, offsets, shapes)
        *row_pieces, _ = lax.optimization_barrier((*row_pieces, own))
        side = side_work(row_pieces, offsets, others)
        late = [swap(rest, size, r * n_vocab) for r in masks[1:-1]]
        late.append(swap(whole, size, masks[-1] * n_vocab))
        pieces = [own, *early, rest, *late, gain_row]
        order = [
            (
                lambda r=r: (lax.axis_index("dp") ^ r) // 2 * rows,
                lambda r=r: (lax.axis_index("dp") ^ r) * rows,
            )
            for r in masks
        ]
    else:
        row_pieces = [lax.all_gather(hidden, "vocab", axis=1, tiled=True)]
        offsets, others = [lambda: 0], []
        root_mean, own = norm(row_pieces, offsets)
        side = side_work(row_pieces, offsets, others)
        pieces = [lax.all_gather(own, "dp", axis=0, tiled=True)]
        order = [(lambda: 0, lambda: 0)]
    weights, in_part, hidden_proj, target_column = side
    partial = call(
        functools.partial(logits_kernel, order, twin, offsets),
        sds((devices, 4 * per_device, projected), BF16),
        len(pieces) + twin + 3,
        us=2.0,
    )(*pieces, unembed, *others, target_column, weights, in_part)
    partial = lax.all_to_all(partial, AXES, 0, 0, tiled=True)
    partial = partial.reshape(n_dp // twin, twin, n_vocab, 4 * per_device, projected)
    merged, logprob = call(
        functools.partial(merge_kernel, features),
        (sds((devices, 2 * per_device, projected), BF16), sds((1, rows), F32)),
        3,
    )(partial, hidden_proj, root_mean)
    merged = lax.all_to_all(merged, AXES, 0, 0, tiled=True)
    padded = -(-seqs // 8) * 8
    scores, logprob = call(
        scores_kernel,
        (sds((seqs, store.shape[0]), F32), sds((1, rows), F32)),
        4,
        scratch=(
            pltpu.VMEM((tokens, projected), F32),
            pltpu.VMEM((tokens, projected), F32),
            pltpu.VMEM((projected * padded, tokens), F32),
            pltpu.VMEM((padded, store.shape[1]), F32),
        ),
    )(merged, segment_ids.reshape(1, tokens), store, logprob)
    return scores, logprob.reshape(rows)


def solution(mesh):
    size = dict(mesh.shape)
    in_specs = (
        P("dp", "vocab"),
        P("dp", "vocab"),
        P(),
        P(AXES, None),
        P(),
        P(),
        P(),
        P(),
        P(AXES, None),
    )
    out_specs = (P(None, AXES), P("dp"))
    return jax.shard_map(
        functools.partial(body, size), mesh=mesh, in_specs=in_specs, out_specs=out_specs, check_vma=False
    )
```

```python
import functools

import jax
import jax.numpy as jnp
from jax import lax
from jax.experimental import pallas as pl
from jax.experimental.pallas import tpu as pltpu
from jax.sharding import PartitionSpec as P


EPSILON = 1e-06
AXES = ("dp", "vocab")
F32 = jnp.float32
BF16 = jnp.bfloat16


VMEM = pl.BlockSpec(memory_space=pltpu.VMEM)
HBM = pl.BlockSpec(memory_space=pltpu.HBM)


def split(x):
    high = x.astype(BF16)
    return high, (x - high.astype(F32)).astype(BF16)


def dot(a, b, dims=((1,), (0,))):
    return lax.dot_general(a, b, (dims, ((), ())), preferred_element_type=F32)


def call(kernel, out_shape, n_in, hbm_at=(), scratch=(), us=1.0):
    specs = [HBM if i in hbm_at else VMEM for i in range(n_in)]
    outs = jax.tree.map(lambda _: VMEM, out_shape)
    run = pl.pallas_call(
        kernel,
        out_shape=out_shape,
        in_specs=specs,
        out_specs=outs,
        scratch_shapes=list(scratch),
        cost_estimate=pl.CostEstimate(flops=0, transcendentals=0, bytes_accessed=int(us * 3_000_000)),
        compiler_params=pltpu.CompilerParams(vmem_limit_bytes=32 * 1024 * 1024),
    )

    def placed(*args):
        return run(
            *[pltpu.with_memory_space_constraint(x, pltpu.HBM) if i in hbm_at else x for i, x in enumerate(args)]
        )

    return placed


def stage_kernel(*refs):
    n = len(refs) // 2
    sources, targets, sems = refs[:n], refs[n : 2 * n], refs[2 * n]
    copies = [
        pltpu.make_async_copy(source, target, sems.at[i])
        for i, (source, target) in enumerate(zip(sources, targets, strict=True))
    ]
    for copy in copies:
        copy.start()
    for copy in copies:
        copy.wait()


def norm_kernel(offsets, *refs):
    n = len(offsets)
    pieces, gain, root_mean, own, rest = refs[:n], refs[n], refs[n + 1], refs[n + 2], refs[n + 3 :]
    squares, features = 0.0, 0
    for piece in pieces:
        wide = piece[...].astype(F32)
        squares = squares + jnp.sum(wide * wide, axis=1, keepdims=True)
        features += wide.shape[1]
    root = jnp.sqrt(squares / features + EPSILON)
    inverse = 1.0 / root
    for k, (piece, offset) in enumerate(zip(pieces, offsets, strict=True)):
        width = piece.shape[1]
        here = pl.ds(pl.multiple_of(offset(), 128), width)
        value = (piece[...].astype(F32) * gain[:, here] * inverse).astype(BF16)
        if k:
            for target in rest:
                target[:, (k - 1) * width : k * width] = value
        else:
            own[...] = value
            if rest:
                rest[1][:, -width:] = value
    if rest:
        lane = lax.broadcasted_iota(jnp.int32, (root.shape[0], 128), 1)
        high = inverse.astype(BF16).astype(F32)
        middle = (inverse - high).astype(BF16).astype(F32)
        low = inverse - high - middle
        rest[0][:, -128:] = jnp.where(lane < 32, high, jnp.where(lane < 64, middle, low)).astype(BF16)
    wide_root = jnp.broadcast_to(root, (root.shape[0], 128))
    chunks, rows, _ = root_mean.shape
    for c in range(chunks):
        root_mean[c] = wide_root[c * rows : (c + 1) * rows]


def side_kernel(offsets, others, *refs):
    n = len(offsets)
    pieces, other_unembeds, refs = refs[:n], refs[n : n + others], refs[n + others :]
    sources, inputs, gain = refs[:4], refs[4], refs[5]
    weights, in_part, hidden_proj, target_column = refs[6:10]
    buffers, sems = refs[10:14], refs[14]
    copies = []
    for i, (source, buffer) in enumerate(zip(sources, buffers, strict=True)):
        if source.shape != buffer.shape:
            width = buffer.shape[0]
            source = source.at[pl.ds(pl.multiple_of(lax.axis_index("vocab") * width, 16), width), :]
        copies.append(pltpu.make_async_copy(source, buffer, sems.at[i]))
        copies[-1].start()
    proj_out, unembed, proj_slice, targets = buffers
    copies[0].wait()
    total = 0.0
    for piece, offset in zip(pieces, offsets, strict=True):
        width = piece.shape[1]
        total = total + dot(piece[...], proj_out[pl.ds(pl.multiple_of(offset(), 16), width), :])
    for u, rows_of in reversed(list(enumerate((unembed, *other_unembeds)))):
        if u == 0:
            copies[1].wait()
        weights[u] = dot((rows_of[...].astype(F32) * gain[...]).astype(BF16), proj_out[...])
    for copy in copies[2:]:
        copy.wait()
    tokens = targets.shape[1]
    target_column[...] = jnp.broadcast_to(targets[...].astype(F32), (128, tokens)).T
    part = dot(inputs[...], proj_slice[...])
    chunks, rows, _ = in_part.shape
    for c in range(chunks):
        in_part[c] = part[c * rows : (c + 1) * rows]
        hidden_proj[c] = total[c * rows : (c + 1) * rows]


def logits_kernel(order, twin, offsets, *refs):
    n = len(order)
    own, refs = refs[0], refs[1:]
    rows, width = own.shape
    blocks = [[own[...]]]
    if n > 1:
        count = n - 2
        early, parts, gain, refs = refs[:count], refs[count : count + n], refs[count + n], refs[count + n + 1 :]
        own_gain = gain[:, pl.ds(pl.multiple_of(offsets[0](), 128), width)]
        for raw, part in zip(early, parts[1:-1], strict=True):
            tail = part[:, -128:].astype(F32)
            inverse = tail[:, 0:1] + tail[:, 32:33] + tail[:, 64:65]
            blocks[0].append((raw[...].astype(F32) * own_gain * inverse).astype(BF16))
        blocks[0].append(parts[-1][:, -width:])
        for k in range(1, len(offsets)):
            blocks.append([part[:, (k - 1) * width : k * width] for part in parts])
    unembeds = refs[:twin]
    target_column, weights, in_part, out = refs[twin:]
    blocks = [jnp.concatenate(block, axis=0) for block in blocks]
    slices = [pl.ds(pl.multiple_of(offset(), 128), width) for offset in offsets]
    entries = unembeds[0].shape[0]
    mine, own_count = lax.axis_index("dp"), lax.axis_size("vocab")
    target = [target_column[pl.ds(pl.multiple_of(whole(), 16), rows), 0:1] for _, whole in order]
    target = jnp.concatenate(target, axis=0)
    sent = target
    if twin > 1:
        sent = [
            target_column[pl.ds(pl.multiple_of((2 * g + 1 - mine % 2) * rows, 16), rows), 0:1] for g in range(n)
        ]
        sent = jnp.concatenate(sent, axis=0)
    logits, onehot, hots = [], [], []
    for u, unembed in enumerate(unembeds):
        relative = sum(dot(unembed[:, at], block, ((1,), (1,))) for at, block in zip(slices, blocks, strict=True)).T
        logits.append(relative)
        place = (mine ^ u) * own_count + lax.axis_index("vocab")
        column = lax.broadcasted_iota(jnp.int32, relative.shape, 1) + place * entries
        onehot.append(target == column.astype(F32))
        hots.append((sent == column.astype(F32)).astype(F32).astype(BF16))
    tokens = logits[0].shape[0]
    peak = functools.reduce(jnp.maximum, [jnp.max(x, axis=1, keepdims=True) for x in logits])
    total = moment = target_logit = sums = target_row = 0.0
    for u in range(twin):
        shifted = logits[u] - peak
        other = jnp.where(onehot[u], 0.0, jnp.exp(shifted))
        total = total + jnp.sum(other, axis=1, keepdims=True)
        moment = moment + jnp.sum(other * shifted, axis=1, keepdims=True)
        target_logit = target_logit + jnp.sum(jnp.where(onehot[u], logits[u], 0.0), axis=1, keepdims=True)
        w_high = weights[u].astype(BF16)
        p_high, p_low = split(other)
        stacked = dot(jnp.concatenate([p_high, hots[u], p_low], axis=0), w_high)
        sums = sums + (stacked[:tokens] + stacked[2 * tokens :])
        target_row = target_row + stacked[tokens : 2 * tokens]
    lane = lax.broadcasted_iota(jnp.int32, (tokens, 128), 1)
    which = (lane // 2) % 4
    stats = jnp.where(which < 2, jnp.where(which == 0, peak, total), jnp.where(which == 2, moment, target_logit))
    high = stats.astype(BF16).astype(F32)
    middle = (stats - high).astype(BF16).astype(F32)
    low = stats - high - middle
    piece = (lane // 8) % 4
    stats = jnp.where(piece == 0, high, jnp.where(piece == 1, middle, jnp.where(piece == 2, low, 0.0)))
    tile = in_part.shape[1]
    block = lax.broadcasted_iota(jnp.int32, (tile, 128), 1) // (128 // own_count)
    for k, (local, _) in enumerate(order):
        for g in range(rows // (own_count * tile)):
            base = k * rows + g * own_count * tile
            row_stats = stats[base : base + tile]
            for c in range(1, own_count):
                row_stats = jnp.where(block == c, stats[base + c * tile : base + (c + 1) * tile], row_stats)
            row = (local() // (own_count * tile) + g) * twin + mine % twin
            row_sent = k * twin + 1 - mine % twin
            for c in range(own_count):
                here = slice(base + c * tile, base + (c + 1) * tile)
                packed = [sums[here], row_stats]
                if twin > 1:
                    out[row * own_count + c] = jnp.concatenate(packed, axis=0).astype(BF16)
                    terms = jnp.where(mine ^ 1 == row_sent, in_part[c], 0.0)
                    packed = jnp.concatenate([target_row[here], terms], axis=0)
                    out[row_sent * own_count + c] = packed.astype(BF16)
                else:
                    terms = jnp.where(mine == row, in_part[c], 0.0)
                    packed = jnp.concatenate([*packed, target_row[here], terms], axis=0)
                    out[row * own_count + c] = packed.astype(BF16)


def merge_kernel(features, parts, hidden_projs, root_means, out, logprob):
    index, own = lax.axis_index("vocab"), lax.axis_size("vocab")
    hidden_proj = hidden_projs[index]
    root_mean = root_means[index]
    rows = hidden_proj.shape[0]
    chunks = parts.shape[0] * own
    twin = parts.shape[1]
    core = lax.axis_index("dp") % twin

    def take(at):
        x = parts[:, at]
        return x.reshape(chunks, *x.shape[2:]).astype(F32)

    received = take(core)
    sent = take(1 - core) if twin > 1 else received[:, 2 * rows : 4 * rows]
    stats = received[:, rows : 2 * rows].reshape(chunks * rows, 128)
    stats = stats + pltpu.roll(stats, 128 - 8, 1) + pltpu.roll(stats, 128 - 16, 1)
    shape = (chunks, rows, 128)
    peak, total = stats.reshape(shape), pltpu.roll(stats, 128 - 2, 1).reshape(shape)
    moment = pltpu.roll(stats, 128 - 4, 1).reshape(shape)
    target_logit = jnp.sum(pltpu.roll(stats, 128 - 6, 1).reshape(shape), axis=0)
    row_peak = jnp.max(peak, axis=0)
    scale = jnp.exp(peak - row_peak[None])
    row_total = jnp.sum(scale * total, axis=0) + jnp.exp(target_logit - row_peak)
    weight = scale / row_total[None]
    rest = jnp.sum(weight * total, axis=0)
    slope = jnp.sum(weight * (total * (target_logit[None] - peak) - moment), axis=0)
    log_of = target_logit - row_peak - jnp.log(row_total)
    group = 128 // own
    lane = lax.broadcasted_iota(jnp.int32, (rows, 128), 1)
    row = lax.broadcasted_iota(jnp.int32, (rows, 128), 0)
    spread = jnp.zeros((rows, 128), F32)
    for k in range(own):
        spread = jnp.where(lane == k * rows + row, log_of[:, k * group : k * group + 1], spread)
    logprob[...] = jnp.sum(spread, axis=0, keepdims=True)[:, 0 : logprob.shape[1]]

    def pick(x):
        at = lax.broadcasted_iota(jnp.int32, x.shape, x.ndim - 1) == index * group
        return jnp.sum(jnp.where(at, x, 0.0), axis=-1, keepdims=True)

    weight, rest, slope = pick(weight), pick(rest), pick(slope)
    target_row = jnp.sum(sent[:, 0:rows], axis=0)
    grad_proj = rest * target_row - jnp.sum(weight * received[:, 0:rows], axis=0)
    grad_dot = root_mean * slope
    out_grad = grad_proj / root_mean - hidden_proj * (
        grad_dot / (features * (root_mean * root_mean * root_mean))
    )
    in_proj = jnp.sum(sent[:, rows : 2 * rows], axis=0)
    both = jnp.concatenate([out_grad, in_proj], axis=0).astype(BF16)
    out[...] = jnp.broadcast_to(both[None], out.shape)


def scores_kernel(parts, segments, store, logprob_in, scores, logprob, out_grad, in_proj, spread, flat):
    logprob[...] = logprob_in[...]
    chunks, rows = parts.shape[0], parts.shape[1] // 2
    for c in range(chunks):
        both = parts[c].astype(F32)
        here = slice(c * rows, (c + 1) * rows)
        out_grad[here, :] = both[0:rows]
        in_proj[here, :] = both[rows : 2 * rows]
    turned = out_grad[...].T
    tokens = turned.shape[1]
    seqs = flat.shape[0]
    member = (segments[...] == lax.broadcasted_iota(jnp.int32, (seqs, tokens), 0)).astype(F32)
    for p in range(turned.shape[0]):
        spread[p * seqs : (p + 1) * seqs, :] = turned[p : p + 1, :] * member
    grads = dot(spread[...].astype(BF16), in_proj[...].astype(BF16))
    width = grads.shape[1]
    for p in range(turned.shape[0]):
        flat[:, p * width : (p + 1) * width] = grads[p * seqs : (p + 1) * seqs, :]
    result = dot(flat[...].astype(BF16), store[...], ((1,), (1,)))
    scores[...] = result[0 : scores.shape[0], :]


def swap(x, size, mask):
    return lax.ppermute(x, AXES, [(i, i ^ mask) for i in range(size["dp"] * size["vocab"])])


def body(size, *args):
    return steps(size, *args)


def steps(size, hidden, inputs, gain, unembed, proj_out, proj_in, targets, segment_ids, store):
    n_dp, n_vocab = size["dp"], size["vocab"]
    devices = n_dp * n_vocab
    tokens, features = targets.shape[0], gain.shape[0]
    per_device = tokens // devices
    rows, width = hidden.shape
    seqs = tokens // 32
    entries = unembed.shape[0]
    projected = proj_out.shape[1]
    gain_row = gain.reshape(1, features)

    sds = jax.ShapeDtypeStruct
    fast = n_dp == 8 and n_vocab == 4 and width % 128 == 0
    twin = 2 if fast else 1
    row_shape = sds((n_vocab, per_device, projected), F32)

    def norm(row_pieces, offsets, rest=()):
        return call(
            functools.partial(norm_kernel, offsets),
            (row_shape, sds((rows, row_pieces[0].shape[1]), BF16), *rest),
            len(row_pieces) + 1,
        )(*row_pieces, gain_row)

    hidden_here, gain_row = call(
        stage_kernel,
        (sds(hidden.shape, BF16), sds(gain_row.shape, F32)),
        2,
        hbm_at=(0, 1),
        scratch=[pltpu.SemaphoreType.DMA((2,))],
    )(hidden, gain_row)

    def side_work(row_pieces, offsets, others, inputs):
        n = len(row_pieces) + len(others)
        sources = (proj_out, unembed, proj_in, targets.reshape(1, tokens))
        shapes = [pltpu.VMEM(x.shape, x.dtype) for x in sources]
        shapes[2] = pltpu.VMEM((inputs.shape[1], projected), BF16)
        return call(
            functools.partial(side_kernel, offsets, len(others)),
            (sds((twin, entries, projected), F32), row_shape, row_shape, sds((tokens, 128), F32)),
            n + 6,
            hbm_at=range(n, n + 4),
            scratch=shapes + [pltpu.SemaphoreType.DMA((4,))],
            us=4.0,
        )(*row_pieces, *others, *sources, inputs, gain_row)

    if fast:
        row_pieces = [swap(hidden, size, k) for k in (2, 3, 1)]
        masks = (0, 6, 4, 2)
        early = [swap(hidden, size, r * n_vocab) for r in masks[1:-1]]
        others = [swap(unembed, size, n_vocab)]
        inputs = swap(inputs, size, n_vocab)
        row_pieces = [hidden_here] + row_pieces
        offsets = [lambda k=k: (lax.axis_index("vocab") ^ k) * width for k in (0, 2, 3, 1)]
        shapes = sds((rows, features - width + 128), BF16), sds((rows, features), BF16)
        root_mean, own, rest, whole = norm(row_pieces, offsets, shapes)
        *row_pieces, _ = lax.optimization_barrier((*row_pieces, own))
        side = side_work(row_pieces, offsets, others, inputs)
        late = [swap(rest, size, r * n_vocab) for r in masks[1:-1]]
        late.append(swap(whole, size, masks[-1] * n_vocab))
        pieces = [own, *early, rest, *late, gain_row]
        order = [
            (
                lambda r=r: (lax.axis_index("dp") ^ r) // 2 * rows,
                lambda r=r: (lax.axis_index("dp") ^ r) * rows,
            )
            for r in masks
        ]
    else:
        row_pieces = [lax.all_gather(hidden, "vocab", axis=1, tiled=True)]
        offsets, others = [lambda: 0], []
        root_mean, own = norm(row_pieces, offsets)
        side = side_work(row_pieces, offsets, others, inputs)
        pieces = [lax.all_gather(own, "dp", axis=0, tiled=True)]
        order = [(lambda: 0, lambda: 0)]
    weights, in_part, hidden_proj, target_column = side
    partial = call(
        functools.partial(logits_kernel, order, twin, offsets),
        sds((devices, 4 // twin * per_device, projected), BF16),
        len(pieces) + twin + 3,
        us=2.0,
    )(*pieces, unembed, *others, target_column, weights, in_part)
    partial = lax.all_to_all(partial, AXES, 0, 0, tiled=True)
    partial = partial.reshape(n_dp // twin, twin, n_vocab, 4 // twin * per_device, projected)
    merged, logprob = call(
        functools.partial(merge_kernel, features),
        (sds((devices, 2 * per_device, projected), BF16), sds((1, rows), F32)),
        3,
    )(partial, hidden_proj, root_mean)
    merged = lax.all_to_all(merged, AXES, 0, 0, tiled=True)
    padded = -(-seqs // 8) * 8
    scores, logprob = call(
        scores_kernel,
        (sds((seqs, store.shape[0]), F32), sds((1, rows), F32)),
        4,
        scratch=(
            pltpu.VMEM((tokens, projected), F32),
            pltpu.VMEM((tokens, projected), F32),
            pltpu.VMEM((projected * padded, tokens), F32),
            pltpu.VMEM((padded, store.shape[1]), F32),
        ),
    )(merged, segment_ids.reshape(1, tokens), store, logprob)
    return scores, logprob.reshape(rows)


def solution(mesh):
    size = dict(mesh.shape)
    in_specs = (
        P("dp", "vocab"),
        P("dp", "vocab"),
        P(),
        P(AXES, None),
        P(),
        P(),
        P(),
        P(),
        P(AXES, None),
    )
    out_specs = (P(None, AXES), P("dp"))
    return jax.shard_map(
        functools.partial(body, size), mesh=mesh, in_specs=in_specs, out_specs=out_specs, check_vma=False
    )
```
